128 devices in a mesh: lat: 8 (over x, y_lo), lon: 16 (over z, y_hi, core).
Axes of the slice: x: 4, y: 4 (y_hi: 2, y_lo: 2; y = y_hi * 2 + y_lo), z: 4, core: 2. Of those that a mesh axis runs over, the one named last changes fastest.
Arguments:
- fine_tokens: bfloat16 [128, 2048, 512], P('lat', 'lon'), may hold values from -6 to 6
- latents: bfloat16 [64, 1024, 512], P('lat', 'lon'), may hold values from -6 to 6
- upsample_weight: bfloat16 [8192, 512], replicated, may hold values from -0.125 to 0.125
- uniting_in: bfloat16 [1024, 1024], replicated, may hold values from -0.1875 to 0.1875
- uniting_out: bfloat16 [1024, 512], replicated, may hold values from -0.1875 to 0.1875
- cotangent: bfloat16 [128, 2048, 512], P('lat', 'lon'), may hold values from -6 to 6
Outputs:
- united: bfloat16 [128, 2048, 512], P('lat', 'lon')
- latent_grad: float32 [64, 1024, 512], P('lat', 'lon')
- uniting_in_grad: float32 [1024, 1024], P('lon', 'lat')
- uniting_out_grad: float32 [1024, 512], P('lon', 'lat')
The draws below stay inside these ranges and needn't reach their ends.
All inputs are finite; a program needn't handle non-finite values.
Results may differ from the reference program's by a relative error of at most 0.014.
Values may be sent and summed in bfloat16 or wider, within the bound.
No kernel may reach another device: no remote copies, remote signals or barrier semaphores. Data moves between devices by JAX's collectives and lax.ppermute only.
A program may use at most 128 MiB of HBM per device.

```python
import jax
import jax.numpy as jnp

D = 512
C = 512
H = 1024
LH = 64
LW = 1024
HH = 128
HW = 2048


def with_spikes(values, key, source, target, blocks, factor):
    def block_of(dim):
        return (jnp.arange(values.shape[dim]) // (values.shape[dim] // blocks)).reshape((-1,) + (1,) * (values.ndim - 1 - dim))

    near = jax.random.permutation(key, blocks)[block_of(target)]
    second = (block_of(target) + blocks // 2) % blocks
    return jnp.where((block_of(source) == near) | (block_of(source) == second), factor * values, values)


def level_of(own_key, shape, split, low, largest):
    def one(dim, parts):
        draws = jax.random.uniform(jax.random.fold_in(jax.random.fold_in(own_key, 6), dim), (parts,), jnp.float32, low / len(split), largest / len(split))
        return jnp.repeat(jnp.exp(draws), shape[dim] // parts).reshape((-1,) + (1,) * (len(shape) - dim - 1))

    factor_of = one(*split[0])
    for cut in split[1:]:
        factor_of = factor_of * one(*cut)
    return factor_of


def noise(stream_key, extent, scale, limit, split=(), dtype=jnp.bfloat16):
    array = jax.random.normal(stream_key, extent, jnp.float32) * scale
    if len(split) > 0:
        array = level_of(stream_key, extent, split, -0.22, 0.18) * array
    return jnp.clip(array, min=-limit, max=limit).astype(dtype)


def heavy_noise(own_key, shape, deviation, limit, pieces, heavy, kind=jnp.bfloat16):
    values = deviation * jax.random.normal(own_key, shape, jnp.float32)
    if pieces:
        values = values * level_of(own_key, shape, pieces, -0.22, 0.18)
    return jnp.clip(with_spikes(values, jax.random.fold_in(own_key, 3), *heavy), -limit, limit).astype(kind)


def setup_inputs(seed: int = 0) -> dict:
    streams_of = jax.random.split(jax.random.key(seed), 7)
    return {
        "fine_tokens": heavy_noise(streams_of[0], (HH, HW, D), 1.0, 6.0, ((0, 8), (1, 16)), (1, 2, 16, 2.0)),
        "latents": noise(streams_of[1], (LH, LW, C), 1.0, 6.0, ((0, 8), (1, 16))),
        "upsample_weight": noise(streams_of[2], (16 * D, C), (4 * C) ** -0.5, 0.125),
        "uniting_in": noise(streams_of[3], (2 * D, H), (2 * D) ** -0.5, 0.1875),
        "uniting_out": noise(streams_of[4], (H, D), H ** -0.5, 0.1875),
        "cotangent": heavy_noise(streams_of[5], (HH, HW, D), 1.0, 6.0, ((0, 8), (1, 16)), (0, 2, 8, 2.0)),
    }


ROW_STEP = (1, 0, 0, -1)
ROW_PARITY = (1, 0, 1, 0)


def shift_field(field, row_step, col_step):
    field_rows = field.shape[0]
    padded = jnp.pad(field, ((1, 1), (0, 0), (0, 0)))
    moved = padded[1 + row_step:1 + row_step + field_rows]
    return jnp.roll(moved, -col_step, axis=1)


def assemble_grid(parity_blocks):
    upper = jnp.stack([parity_blocks[0][0], parity_blocks[0][1]], axis=2)
    lower = jnp.stack([parity_blocks[1][0], parity_blocks[1][1]], axis=2)
    stacked = jnp.stack([upper, lower], axis=1)
    dims = stacked.shape
    return stacked.reshape(dims[0] * 2, dims[2] * 2, dims[4])


def reference(fine_tokens, latents, upsample_weight, uniting_in, uniting_out, cotangent):
    lat_rows, lat_cols, latent_width = latents.shape
    model_width = fine_tokens.shape[2]
    kernels = upsample_weight.reshape(16, model_width, latent_width)
    sums = [[jnp.zeros((lat_rows * lat_cols, model_width), jnp.float32) for parity_col in range(2)] for parity_row in range(2)]
    for kernel_row in range(4):
        for kernel_col in range(4):
            source = shift_field(latents, ROW_STEP[kernel_row], ROW_STEP[kernel_col]).reshape(-1, latent_width)
            term = jnp.dot(source, kernels[kernel_row * 4 + kernel_col].T, preferred_element_type=jnp.float32)
            parity_row = ROW_PARITY[kernel_row]
            parity_col = ROW_PARITY[kernel_col]
            sums[parity_row][parity_col] = sums[parity_row][parity_col] + term
    blocks = [[sums[parity_row][parity_col].reshape(lat_rows, lat_cols, model_width).astype(jnp.bfloat16) for parity_col in range(2)] for parity_row in range(2)]
    upsampled = assemble_grid(blocks)
    token_count = fine_tokens.shape[0] * fine_tokens.shape[1]
    tokens = fine_tokens.reshape(token_count, model_width)
    joined = jnp.concatenate([tokens, upsampled.reshape(token_count, model_width)], axis=1)
    hidden_pre = jnp.dot(joined, uniting_in, preferred_element_type=jnp.float32)
    activation = jax.nn.silu(hidden_pre).astype(jnp.bfloat16)
    united = (tokens.astype(jnp.float32) + jnp.dot(activation, uniting_out, preferred_element_type=jnp.float32)).astype(jnp.bfloat16)
    upstream = cotangent.reshape(token_count, model_width)
    act_grad = jnp.dot(upstream, uniting_out.T, preferred_element_type=jnp.float32)
    sigmoid_gate = jax.nn.sigmoid(hidden_pre)
    pre_grad = (act_grad * sigmoid_gate * (1.0 + hidden_pre * (1.0 - sigmoid_gate))).astype(jnp.bfloat16)
    uniting_out_grad = jnp.dot(activation.T, upstream, preferred_element_type=jnp.float32)
    uniting_in_grad = jnp.dot(joined.T, pre_grad, preferred_element_type=jnp.float32)
    up_cot = jnp.dot(pre_grad, uniting_in[model_width:].T, preferred_element_type=jnp.float32).astype(jnp.bfloat16)
    up_cot = up_cot.reshape(fine_tokens.shape)
    latent_grad = jnp.zeros((lat_rows, lat_cols, latent_width), jnp.float32)
    for kernel_row in range(4):
        for kernel_col in range(4):
            parity_part = up_cot[ROW_PARITY[kernel_row]::2, ROW_PARITY[kernel_col]::2]
            moved = shift_field(parity_part, -ROW_STEP[kernel_row], -ROW_STEP[kernel_col]).reshape(-1, model_width)
            term = jnp.dot(moved, kernels[kernel_row * 4 + kernel_col], preferred_element_type=jnp.float32)
            latent_grad = latent_grad + term.reshape(lat_rows, lat_cols, latent_width)
    return united.reshape(fine_tokens.shape), latent_grad, uniting_in_grad, uniting_out_grad
```

```python
import jax
import jax.numpy as jnp
from jax import lax
from jax.sharding import PartitionSpec as P

ROW_STEP = (1, 0, 0, -1)
ROW_PARITY = (1, 0, 1, 0)


def with_halo(array, sides, width, wrap):
    for axis, dim in sides:
        devices, length = (lax.axis_size(axis), array.shape[dim])
        up = [(i, (i + 1) % devices) for i in range(devices if wrap else devices - 1)]
        down = [(j, i) for i, j in up]
        last = lax.slice_in_dim(array, length - width, length, axis=dim)
        first = lax.slice_in_dim(array, 0, width, axis=dim)
        before = lax.ppermute(last, axis, up)
        after = lax.ppermute(first, axis, down)
        array = jnp.concatenate([before, array, after], axis=dim)
    return array


def extend_latents(latents):
    row_extended = with_halo(latents, (("lat", 0),), 1, False)
    extended = with_halo(row_extended, (("lon", 1),), 1, True)
    return extended


def extend_cotangent(up_cot):
    row_extended = with_halo(up_cot, (("lat", 0),), 1, False)
    extended = with_halo(row_extended, (("lon", 1),), 1, True)
    return extended


def assemble_grid(parity_blocks):
    upper = jnp.stack([parity_blocks[0][0], parity_blocks[0][1]], axis=2)
    lower = jnp.stack([parity_blocks[1][0], parity_blocks[1][1]], axis=2)
    stacked = jnp.stack([upper, lower], axis=1)
    dims = stacked.shape
    return stacked.reshape(dims[0] * 2, dims[2] * 2, dims[4])

BOTH = ("lat", "lon")


def device_index(x, y_lo, z, y_hi, core):
    return (x * 2 + y_lo) * 16 + z * 4 + y_hi * 2 + core


def chip_groups():
    return [
        [
            device_index(x, y_lo, z, y_hi, core)
            for z in range(4)
            for x in range(4)
            for y_hi in range(2)
            for y_lo in range(2)
        ]
        for core in range(2)
    ]


def pack_in(grad):
    split = grad.astype(jnp.bfloat16).reshape(4, 2, 2, 64, 4, 2, 128)
    return split.transpose(2, 0, 4, 1, 5, 3, 6).reshape(2, 64, 64, 128)


def pack_out(grad):
    split = grad.astype(jnp.bfloat16).reshape(4, 2, 2, 2, 32, 4, 2, 64)
    return split.transpose(2, 0, 5, 1, 6, 4, 3, 7).reshape(2, 64, 32, 128)


def reduce_blocks(blocks):
    core = lax.axis_index("lon") % 2
    pairs = [(i, i ^ 1) for i in range(16)]
    other = lax.ppermute(
        lax.dynamic_index_in_dim(blocks, 1 - core, 0, keepdims=False), "lon", pairs
    )
    own = lax.dynamic_index_in_dim(blocks, core, 0, keepdims=False)
    halves = (own.astype(jnp.float32) + other.astype(jnp.float32)).astype(jnp.bfloat16)
    received = lax.all_to_all(
        halves, BOTH, 0, 0, axis_index_groups=chip_groups(), tiled=True
    )
    total = jnp.sum(received.astype(jnp.float32), axis=0)
    out_grad = total[64:].reshape(32, 2, 64).transpose(1, 0, 2).reshape(64, 64)
    return total[:64], out_grad


def shards(fine_tokens, latents, upsample_weight, uniting_in, uniting_out, cotangent):
    lat_rows, lat_cols, latent_width = latents.shape
    model_width = fine_tokens.shape[2]
    latent_ext = extend_latents(latents)
    kernels = upsample_weight.reshape(16, model_width, latent_width)
    parity_blocks = []
    for parity_row in range(2):
        block_row = []
        for parity_col in range(2):
            summed = jnp.zeros((lat_rows, lat_cols, model_width), jnp.float32)
            for kernel_row in range(4):
                for kernel_col in range(4):
                    if (
                        ROW_PARITY[kernel_row] == parity_row
                        and ROW_PARITY[kernel_col] == parity_col
                    ):
                        row_start = 1 + ROW_STEP[kernel_row]
                        col_start = 1 + ROW_STEP[kernel_col]
                        source = latent_ext[
                            row_start : row_start + lat_rows, col_start : col_start + lat_cols
                        ]
                        summed = summed + lax.dot_general(
                            source,
                            kernels[kernel_row * 4 + kernel_col],
                            (((2,), (1,)), ((), ())),
                            preferred_element_type=jnp.float32,
                        )
            block_row.append(summed.astype(jnp.bfloat16))
        parity_blocks.append(block_row)
    upsampled = assemble_grid(parity_blocks)
    token_count = fine_tokens.shape[0] * fine_tokens.shape[1]
    tokens = fine_tokens.reshape(token_count, model_width)
    joined = jnp.concatenate([tokens, upsampled.reshape(token_count, model_width)], axis=1)
    hidden_pre = jnp.dot(joined, uniting_in, preferred_element_type=jnp.float32)
    activation = jax.nn.silu(hidden_pre).astype(jnp.bfloat16)
    united = (
        tokens.astype(jnp.float32)
        + jnp.dot(activation, uniting_out, preferred_element_type=jnp.float32)
    ).astype(jnp.bfloat16)
    upstream = cotangent.reshape(token_count, model_width)
    act_grad = lax.dot_general(
        upstream, uniting_out, (((1,), (1,)), ((), ())), preferred_element_type=jnp.float32
    )
    sigmoid_gate = jax.nn.sigmoid(hidden_pre)
    pre_grad = (act_grad * sigmoid_gate * (1.0 + hidden_pre * (1.0 - sigmoid_gate))).astype(
        jnp.bfloat16
    )
    out_local = lax.dot_general(
        activation, upstream, (((0,), (0,)), ((), ())), preferred_element_type=jnp.float32
    )
    in_local = lax.dot_general(
        joined, pre_grad, (((0,), (0,)), ((), ())), preferred_element_type=jnp.float32
    )
    blocks = jnp.concatenate([pack_in(in_local), pack_out(out_local)], axis=2)
    uniting_in_grad, uniting_out_grad = reduce_blocks(blocks)
    up_cot = lax.dot_general(
        pre_grad,
        uniting_in[model_width:],
        (((1,), (1,)), ((), ())),
        preferred_element_type=jnp.float32,
    )
    up_cot = up_cot.astype(jnp.bfloat16).reshape(fine_tokens.shape)
    cot_ext = extend_cotangent(up_cot)
    split_grid = cot_ext.reshape(lat_rows + 1, 2, lat_cols + 1, 2, model_width).transpose(
        1, 3, 0, 2, 4
    )
    latent_grad = jnp.zeros((lat_rows, lat_cols, latent_width), jnp.float32)
    for kernel_row in range(4):
        for kernel_col in range(4):
            row_start = 1 + ROW_PARITY[kernel_row] - 2 * ROW_STEP[kernel_row]
            col_start = 1 + ROW_PARITY[kernel_col] - 2 * ROW_STEP[kernel_col]
            window = split_grid[
                row_start % 2,
                col_start % 2,
                row_start // 2 : row_start // 2 + lat_rows,
                col_start // 2 : col_start // 2 + lat_cols,
            ]
            latent_grad = latent_grad + lax.dot_general(
                window,
                kernels[kernel_row * 4 + kernel_col],
                (((2,), (0,)), ((), ())),
                preferred_element_type=jnp.float32,
            )
    return (united.reshape(fine_tokens.shape), latent_grad, uniting_in_grad, uniting_out_grad)


def solution(mesh):
    return jax.shard_map(
        shards,
        mesh=mesh,
        in_specs=(
            P("lat", "lon", None),
            P("lat", "lon", None),
            P(),
            P(),
            P(),
            P("lat", "lon", None),
        ),
        out_specs=(P("lat", "lon", None), P("lat", "lon", None), P("lon", "lat"), P("lon", "lat")),
        check_vma=False,
    )
```

```python
import jax
import jax.numpy as jnp
from jax import lax
from jax.experimental import pallas as pl
from jax.experimental.pallas import tpu as pltpu
from jax.sharding import PartitionSpec as P

BF16 = jnp.bfloat16
F32 = jnp.float32
BOTH = ("lat", "lon")


def dot_nn(a, b):
    return lax.dot_general(a, b, (((1,), (0,)), ((), ())), preferred_element_type=F32)


def dot_nt(a, b):
    return lax.dot_general(a, b, (((1,), (1,)), ((), ())), preferred_element_type=F32)


def dot_tn(a, b):
    return lax.dot_general(a, b, (((0,), (0,)), ((), ())), preferred_element_type=F32)


def cost(flops, nbytes):
    return pl.CostEstimate(flops=flops, bytes_accessed=nbytes, transcendentals=0)


def params():
    return pltpu.CompilerParams(vmem_limit_bytes=60 << 20)


def iota(shape, dim):
    return lax.broadcasted_iota(jnp.int32, shape, dim)


def upsample_body(lat, before, after, left, right, w_a, w_b, out, shifts):
    parity, half = pl.program_id(0), pl.program_id(1)
    rows, cols, width = lat.shape

    @pl.when((parity == 0) & (half == 0))
    def _():
        lefts, rights = left[...].astype(F32), right[...].astype(F32)
        place = iota((cols, width), 0)
        for r in range(rows + 2):
            row = before[0] if r == 0 else after[0] if r == rows + 1 else lat[r - 1]
            wide = row.astype(F32)
            shifts[1, r] = row
            shifts[0, r] = jnp.where(
                place == 0, lefts[r : r + 1], pltpu.roll(wide, 1, 0)
            ).astype(BF16)
            shifts[2, r] = jnp.where(
                place == cols - 1, rights[r : r + 1], pltpu.roll(wide, cols - 1, 0)
            ).astype(BF16)

    planes = []
    for taps in (((1, 0), (3, -1)), ((0, 1), (2, 0))):
        total = None
        for weight, start in ((w_a, 1 + parity), (w_b, parity)):
            for tap, step in taps:
                source = shifts[step + 1, pl.ds(start, rows)].reshape(rows * cols, width)
                term = dot_nt(source, weight[0, tap])
                total = term if total is None else total + term
        planes.append(total.astype(BF16))
    size = 2 * cols
    r, k = iota((size, size), 0), iota((size, size), 1)
    spread = (k == (r % 2) * cols + r // 2).astype(F32).astype(BF16)
    for m in range(rows):
        pair = jnp.concatenate([z[m * cols : (m + 1) * cols] for z in planes], axis=0)
        out[m, 0] = dot_nn(spread, pair).astype(BF16)


def upsample(lat, before, after, left, right, weight):
    rows, cols, width = lat.shape
    model = weight.shape[0] // 16
    half = model // 2
    whole = lambda *shape: pl.BlockSpec(shape, lambda p, h: (0,) * len(shape))
    return pl.pallas_call(
        upsample_body,
        grid=(2, 2),
        in_specs=[
            whole(rows, cols, width),
            whole(1, cols, width),
            whole(1, cols, width),
            whole(rows + 2, width),
            whole(rows + 2, width),
            pl.BlockSpec((1, 4, half, width), lambda p, h: (1 - p, 0, h, 0)),
            pl.BlockSpec((1, 4, half, width), lambda p, h: (3 - p, 0, h, 0)),
        ],
        out_specs=pl.BlockSpec((rows, 1, 2 * cols, half), lambda p, h: (0, p, 0, h)),
        out_shape=jax.ShapeDtypeStruct((rows, 2, 2 * cols, model), BF16),
        scratch_shapes=[pltpu.VMEM((3, rows + 2, cols, width), BF16)],
        compiler_params=params(),
        cost_estimate=cost(5 << 30, 12 << 20),
        name="upsample",
    )(lat, before, after, left, right, *[weight.reshape(4, 4, model, width)] * 2)


def middle_body(tokens, up, cot, w_in, w_out, act, pre, up_cot):
    hidden, model = w_out.shape
    step = 256
    for n in range(0, hidden, step):
        cols = slice(n, n + step)
        h = dot_nn(tokens[...], w_in[:model, cols]) + dot_nn(up[...], w_in[model:, cols])
        a = dot_nt(cot[...], w_out[cols, :])
        g = 0.5 * jnp.tanh(0.5 * h) + 0.5
        y = h * g
        act[:, cols] = y.astype(BF16)
        pre[:, cols] = (a * (g + y * (1.0 - g))).astype(BF16)
    up_cot[...] = dot_nt(pre[...], w_in[model:, :]).astype(BF16)


def middle(tokens, up, cot, w_in, w_out):
    count, model = tokens.shape
    hidden = w_out.shape[0]
    block = count // 4
    rows = lambda width: pl.BlockSpec((block, width), lambda i: (i, 0))
    whole = lambda a: pl.BlockSpec(a.shape, lambda i: (0, 0))
    return pl.pallas_call(
        middle_body,
        grid=(4,),
        in_specs=[rows(model)] * 3 + [whole(w_in), whole(w_out)],
        out_specs=[rows(hidden), rows(hidden), rows(model)],
        out_shape=[
            jax.ShapeDtypeStruct((count, hidden), BF16),
            jax.ShapeDtypeStruct((count, hidden), BF16),
            jax.ShapeDtypeStruct((count, model), BF16),
        ],
        compiler_params=params(),
        cost_estimate=cost(10 << 30, 20 << 20),
        name="middle",
    )(tokens, up, cot, w_in, w_out)


def out_grad_body(core, act, cot, keep, send, total):
    total[...] = dot_tn(act[...], cot[...])
    low = iota((32, 128), 1) < 64
    for which, ref in ((core[0], keep), (1 - core[0], send)):
        for y_hi in range(2):
            base = pl.multiple_of(y_hi * 128 + which * 64, 64)
            for x in range(4):
                cols = slice(x * 128, (x + 1) * 128)
                a = total[pl.ds(base, 32), cols]
                b = total[pl.ds(base + 32, 32), cols]
                at = x * 4 + y_hi * 2
                ref[at] = jnp.where(low, a, pltpu.roll(b, 64, 1)).astype(BF16)
                ref[at + 1] = jnp.where(low, pltpu.roll(a, 64, 1), b).astype(BF16)


def out_grad_blocks(core, act, cot):
    count, hidden = act.shape
    model = cot.shape[1]
    spec = pl.BlockSpec((16, 32, 128), lambda j, c: (j, 0, 0))
    return pl.pallas_call(
        out_grad_body,
        grid_spec=pltpu.PrefetchScalarGridSpec(
            num_scalar_prefetch=1,
            grid=(4,),
            in_specs=[
                pl.BlockSpec((count, hidden // 4), lambda j, c: (0, j)),
                pl.BlockSpec((count, model), lambda j, c: (0, 0)),
            ],
            out_specs=[spec, spec],
            scratch_shapes=[pltpu.VMEM((hidden // 4, model), F32)],
        ),
        out_shape=[jax.ShapeDtypeStruct((64, 32, 128), BF16)] * 2,
        compiler_params=params(),
        cost_estimate=cost(2 << 30, 7 << 20),
        name="out_grad",
    )(core, act, cot)


def in_grad_body(core, tokens, up, pre, keep, send, total):
    model = tokens.shape[1]
    total[:model] = dot_tn(tokens[...], pre[...])
    total[model:] = dot_tn(up[...], pre[...])
    for which, ref in ((core[0], keep), (1 - core[0], send)):
        for z in range(4):
            for y_hi in range(2):
                base = pl.multiple_of((z * 2 + y_hi) * 128 + which * 64, 64)
                for y_lo in range(2):
                    ref[z, 0, y_hi * 2 + y_lo] = total[
                        pl.ds(base, 64), y_lo * 128 : (y_lo + 1) * 128
                    ].astype(BF16)


def in_grad_blocks(core, tokens, up, pre):
    count, hidden = pre.shape
    model = tokens.shape[1]
    spec = pl.BlockSpec((4, 1, 4, 64, 128), lambda j, c: (0, j, 0, 0, 0))
    return pl.pallas_call(
        in_grad_body,
        grid_spec=pltpu.PrefetchScalarGridSpec(
            num_scalar_prefetch=1,
            grid=(4,),
            in_specs=[
                pl.BlockSpec((count, model), lambda j, c: (0, 0)),
                pl.BlockSpec((count, model), lambda j, c: (0, 0)),
                pl.BlockSpec((count, hidden // 4), lambda j, c: (0, j)),
            ],
            out_specs=[spec, spec],
            scratch_shapes=[pltpu.VMEM((2 * model, hidden // 4), F32)],
        ),
        out_shape=[jax.ShapeDtypeStruct((4, 4, 4, 64, 128), BF16)] * 2,
        compiler_params=params(),
        cost_estimate=cost(4 << 30, 10 << 20),
        name="in_grad",
    )(core, tokens, up, pre)


def united_body(tokens, act, w_out, out):
    out[...] = (tokens[...].astype(F32) + dot_nn(act[...], w_out[...])).astype(BF16)


def unite(tokens, act, w_out):
    count, model = tokens.shape
    hidden = act.shape[1]
    block = count // 4
    return pl.pallas_call(
        united_body,
        grid=(4,),
        in_specs=[
            pl.BlockSpec((block, model), lambda i: (i, 0)),
            pl.BlockSpec((block, hidden), lambda i: (i, 0)),
            pl.BlockSpec((hidden, model), lambda i: (0, 0)),
        ],
        out_specs=pl.BlockSpec((block, model), lambda i: (i, 0)),
        out_shape=jax.ShapeDtypeStruct((count, model), BF16),
        compiler_params=params(),
        cost_estimate=cost(2 << 30, 9 << 20),
        name="unite",
    )(tokens, act, w_out)


def pair_body(in_a, in_b, out_a, out_b, both):
    both[:, :64] = (in_a[...].astype(F32) + in_b[...].astype(F32)).astype(BF16)
    both[:, 64:] = (out_a[...].astype(F32) + out_b[...].astype(F32)).astype(BF16)


def add_pair(in_a, in_b, out_a, out_b):
    spec = lambda rows: pl.BlockSpec((32, rows, 128), lambda i: (i, 0, 0))
    return pl.pallas_call(
        pair_body,
        grid=(2,),
        in_specs=[spec(64), spec(64), spec(32), spec(32)],
        out_specs=spec(96),
        out_shape=jax.ShapeDtypeStruct((64, 96, 128), BF16),
        compiler_params=params(),
        cost_estimate=cost(1 << 20, 5 << 20),
        name="add_pair",
    )(in_a, in_b, out_a, out_b)


def sum_body(parts, in_grad, out_grad):
    total = parts[0].astype(F32)
    for i in range(1, parts.shape[0]):
        total = total + parts[i].astype(F32)
    in_grad[...] = total[:64]
    out_grad[:32] = total[64:, :64]
    out_grad[32:] = pltpu.roll(total[64:], 64, 1)[:, :64]


def sum_blocks(parts):
    return pl.pallas_call(
        sum_body,
        out_shape=[
            jax.ShapeDtypeStruct((64, 128), F32),
            jax.ShapeDtypeStruct((64, 64), F32),
        ],
        compiler_params=params(),
        cost_estimate=cost(1 << 20, 2 << 20),
        name="sum_blocks",
    )(parts)


def latent_body(cot, before, after, sides, weight, out, planes):
    step = pl.program_id(0)
    fine_rows, fine_cols, model = cot.shape
    cols = fine_cols // 2

    @pl.when(step == 0)
    def _():
        r, c = iota((4 * cols, fine_cols), 0), iota((4 * cols, fine_cols), 1)
        pick = (c == 2 * (r % cols) + r // cols - 1).astype(F32).astype(BF16)
        r, c = iota((4 * cols, 16), 0), iota((4 * cols, 16), 1)
        edge = ((r == 0) & (c == 0)) | ((r == 4 * cols - 1) & (c == 1))
        edge = edge.astype(F32).astype(BF16)
        for e in range(fine_rows + 2):
            row = before[0] if e == 0 else after[0] if e == fine_rows + 1 else cot[e - 1]
            found = (dot_nn(pick, row) + dot_nn(edge, sides[e])).astype(BF16)
            for tap in range(4):
                planes[e % 2, e // 2, :, tap * model : (tap + 1) * model] = found[
                    tap * cols : (tap + 1) * cols
                ]

    rows = fine_rows // 2
    source = planes[step % 2, pl.ds(step // 2, rows)].reshape(rows * cols, 4 * model)
    term = dot_nn(source, weight[0])

    @pl.when(step == 0)
    def _():
        out[...] = term

    @pl.when(step != 0)
    def _():
        out[...] += term


def latent_gradient(cot, before, after, sides, weight):
    fine_rows, fine_cols, model = cot.shape
    width = weight.shape[1]
    whole = lambda a: pl.BlockSpec(a.shape, lambda i: (0, 0, 0))
    size = fine_rows * fine_cols // 4
    return pl.pallas_call(
        latent_body,
        grid=(4,),
        in_specs=[
            whole(cot),
            whole(before),
            whole(after),
            whole(sides),
            pl.BlockSpec((1, 4 * model, width), lambda i: (i, 0, 0)),
        ],
        out_specs=pl.BlockSpec((size, width), lambda i: (0, 0)),
        out_shape=jax.ShapeDtypeStruct((size, width), F32),
        scratch_shapes=[
            pltpu.VMEM((2, fine_rows // 2 + 1, fine_cols // 2, 4 * model), BF16)
        ],
        compiler_params=params(),
        cost_estimate=cost(5 << 30, 12 << 20),
        name="latent_gradient",
    )(cot, before, after, sides, weight.reshape(4, 4 * model, width))


def neighbours(array, axis, dim, wrap):
    devices = lax.axis_size(axis)
    up = [(i, (i + 1) % devices) for i in range(devices if wrap else devices - 1)]
    down = [(j, i) for i, j in up]
    length = array.shape[dim]
    last = lax.slice_in_dim(array, length - 1, length, axis=dim)
    first = lax.slice_in_dim(array, 0, 1, axis=dim)
    return lax.ppermute(last, axis, up), lax.ppermute(first, axis, down)


def side_columns(array, before, after):
    devices = lax.axis_size("lon")
    up = [(i, (i + 1) % devices) for i in range(devices)]
    down = [(j, i) for i, j in up]
    column = lambda c: jnp.concatenate([before[:, c], array[:, c], after[:, c]], axis=0)
    return lax.ppermute(column(-1), "lon", up), lax.ppermute(column(0), "lon", down)


def chip_groups():
    return [
        [
            (x * 2 + y_lo) * 16 + z * 4 + y_hi * 2 + core
            for z in range(4)
            for x in range(4)
            for y_hi in range(2)
            for y_lo in range(2)
        ]
        for core in range(2)
    ]


def other_core(array):
    return lax.ppermute(array, "lon", [(i, i ^ 1) for i in range(16)])


def shards(fine_tokens, latents, upsample_weight, uniting_in, uniting_out, cotangent):
    count = fine_tokens.shape[0] * fine_tokens.shape[1]
    model = fine_tokens.shape[2]
    core = (lax.axis_index("lon") % 2).astype(jnp.int32).reshape(1)
    tokens = fine_tokens.reshape(count, model)
    cot = cotangent.reshape(count, model)

    before, after = neighbours(latents, "lat", 0, False)
    left, right = side_columns(latents, before, after)
    up = upsample(latents, before, after, left, right, upsample_weight)
    up = up.reshape(count, model)
    act, pre, up_cot = middle(tokens, up, cot, uniting_in, uniting_out)

    up_cot = up_cot.reshape(fine_tokens.shape)
    cot_before, cot_after = neighbours(up_cot, "lat", 0, False)
    out_keep, out_send = out_grad_blocks(core, act, cot)
    out_other = other_core(out_send)
    sides = side_columns(up_cot, cot_before, cot_after)
    in_keep, in_send = in_grad_blocks(core, tokens, up, pre)
    in_other = other_core(in_send)
    united = unite(tokens, act, uniting_out)
    flat = lambda a: a.reshape(64, 64, 128)
    halves = add_pair(flat(in_keep), flat(in_other), out_keep, out_other)
    parts = lax.all_to_all(halves, BOTH, 0, 0, axis_index_groups=chip_groups(), tiled=True)

    sides = jnp.pad(jnp.stack(sides, axis=1), ((0, 0), (0, 14), (0, 0)))
    latent_grad = latent_gradient(up_cot, cot_before, cot_after, sides, upsample_weight)
    in_grad, out_grad = sum_blocks(parts)
    return (
        united.reshape(fine_tokens.shape),
        latent_grad.reshape(latents.shape),
        in_grad,
        out_grad,
    )


def solution(mesh):
    return jax.shard_map(
        shards,
        mesh=mesh,
        in_specs=(
            P("lat", "lon", None),
            P("lat", "lon", None),
            P(),
            P(),
            P(),
            P("lat", "lon", None),
        ),
        out_specs=(P("lat", "lon", None), P("lat", "lon", None), P("lon", "lat"), P("lon", "lat")),
        check_vma=False,
    )
```

```python
import jax
import jax.numpy as jnp
from jax import lax
from jax.experimental import pallas as pl
from jax.experimental.pallas import tpu as pltpu
from jax.sharding import PartitionSpec as P

BF16 = jnp.bfloat16
F32 = jnp.float32
BOTH = ("lat", "lon")


def dot_nn(a, b):
    return lax.dot_general(a, b, (((1,), (0,)), ((), ())), preferred_element_type=F32)


def dot_nt(a, b):
    return lax.dot_general(a, b, (((1,), (1,)), ((), ())), preferred_element_type=F32)


def dot_tn(a, b):
    return lax.dot_general(a, b, (((0,), (0,)), ((), ())), preferred_element_type=F32)


def cost(flops, nbytes):
    return pl.CostEstimate(flops=flops, bytes_accessed=nbytes, transcendentals=0)


def params():
    return pltpu.CompilerParams(vmem_limit_bytes=60 << 20)


def iota(shape, dim):
    return lax.broadcasted_iota(jnp.int32, shape, dim)


def main_body(
    core, lat, before, after, left, right, w_a, w_b, h_top, a_top, tokens_hbm, cot_hbm, w_hbm,
    act_out, up_cot, keep, send,
    shifts, tokens, cot, w_low, up, act, pre, turned, sems,
):
    step = pl.program_id(0)
    rows, cols, width = lat.shape
    model, hidden = w_low.shape
    block = h_top.shape[0]
    copies = [
        pltpu.make_async_copy(w_hbm.at[pl.ds(model, model)], w_low, sems.at[0]),
        pltpu.make_async_copy(tokens_hbm, tokens, sems.at[1]),
        pltpu.make_async_copy(cot_hbm, cot, sems.at[2]),
    ]

    @pl.when(step == 0)
    def _():
        for copy in copies:
            copy.start()
        lefts, rights = left[...].astype(F32), right[...].astype(F32)
        place = iota((cols, width), 0)
        for r in range(rows + 2):
            row = before[0] if r == 0 else after[0] if r == rows + 1 else lat[r - 1]
            wide = row.astype(F32)
            shifts[1, r] = row
            shifts[0, r] = jnp.where(
                place == 0, lefts[r : r + 1], pltpu.roll(wide, 1, 0)
            ).astype(BF16)
            shifts[2, r] = jnp.where(
                place == cols - 1, rights[r : r + 1], pltpu.roll(wide, cols - 1, 0)
            ).astype(BF16)

    @pl.when(step < 4)
    def _():
        parity, half = step // 2, step % 2
        planes = []
        for taps in (((1, 0), (3, -1)), ((0, 1), (2, 0))):
            total = None
            for weight, start in ((w_a, 1 + parity), (w_b, parity)):
                for tap, move in taps:
                    source = shifts[move + 1, pl.ds(start, rows)].reshape(rows * cols, width)
                    term = dot_nt(source, weight[0, tap])
                    total = term if total is None else total + term
            planes.append(total.astype(BF16))
        size = 2 * cols
        r, k = iota((size, size), 0), iota((size, size), 1)
        spread = (k == (r % 2) * cols + r // 2).astype(F32).astype(BF16)
        for m in range(rows):
            pair = jnp.concatenate([z[m * cols : (m + 1) * cols] for z in planes], axis=0)
            value = dot_nn(spread, pair).astype(BF16)
            at = pl.ds(pl.multiple_of((2 * m + parity) * size, size), size)
            for side in range(2):
                @pl.when(half == side)
                def _():
                    up[at, side * (model // 2) : (side + 1) * (model // 2)] = value

    @pl.when(step == 4)
    def _():
        for copy in copies:
            copy.wait()

    @pl.when((step >= 4) & (step < 8))
    def _():
        at = pl.ds(pl.multiple_of((step - 4) * block, block), block)
        for n in range(0, hidden, 256):
            span = slice(n, n + 256)
            h = h_top[:, span].astype(F32) + dot_nn(up[at, :], w_low[:, span])
            g = 0.5 * jnp.tanh(0.5 * h) + 0.5
            y = h * g
            wide = y.astype(BF16)
            act[at, span] = wide
            act_out[:, span] = wide
            a = a_top[:, span].astype(F32)
            pre[at, span] = (a * (g + y * (1.0 - g))).astype(BF16)
        up_cot[...] = dot_nt(pre[at, :], w_low[...]).astype(BF16)
        turned[0:model, at] = tokens[at, :].T
        turned[model : 2 * model, at] = up[at, :].T
        turned[2 * model :, at] = cot[at, :].T

    for j in range(4):

        @pl.when(step == 8 + j)
        def _():
            span = slice(j * 256, (j + 1) * 256)
            mine = core[0]
            total = dot_nn(turned[: 2 * model], pre[:, span])
            for z in range(4):
                for y_hi in range(2):
                    base = (z * 2 + y_hi) * 128
                    first, second = total[base : base + 64], total[base + 64 : base + 128]
                    own = jnp.where(mine == 0, first, second).astype(BF16)
                    other = jnp.where(mine == 0, second, first).astype(BF16)
                    for y_lo in range(2):
                        lanes = slice(y_lo * 128, (y_lo + 1) * 128)
                        keep[z, j, y_hi * 2 + y_lo, 0:64] = own[:, lanes]
                        send[z, j, y_hi * 2 + y_lo, 0:64] = other[:, lanes]
            total = dot_nn(turned[2 * model :], act[:, span])
            low = iota((32, 128), 1) < 64
            for lat_id in range(8):
                for y_hi in range(2):
                    lanes = slice(y_hi * 128, (y_hi + 1) * 128)
                    a = total[lat_id * 64 : lat_id * 64 + 32, lanes]
                    b = total[lat_id * 64 + 32 : lat_id * 64 + 64, lanes]
                    first = jnp.where(low, a, pltpu.roll(b, 64, 1))
                    second = jnp.where(low, pltpu.roll(a, 64, 1), b)
                    at = y_hi * 2 + lat_id % 2
                    keep[j, lat_id // 2, at, 64:96] = jnp.where(
                        mine == 0, first, second
                    ).astype(BF16)
                    send[j, lat_id // 2, at, 64:96] = jnp.where(
                        mine == 0, second, first
                    ).astype(BF16)


def main_kernel(core, lat, before, after, left, right, weight, h_top, a_top, tokens, cot, w_in):
    rows, cols, width = lat.shape
    model = weight.shape[0] // 16
    half = model // 2
    count, hidden = h_top.shape
    block = count // 4
    clamp = lambda i, low: jnp.clip(i - low, 0, 3)
    whole = lambda *shape: pl.BlockSpec(shape, lambda i, c: (0,) * len(shape))
    kernel_row = lambda i, top: (top - clamp(i, 0) // 2, 0, clamp(i, 0) % 2, 0)
    tokens_of = lambda w: pl.BlockSpec((block, w), lambda i, c: (clamp(i, 4), 0))
    blocks = (4, 4, 4, 96, 128)
    return pl.pallas_call(
        main_body,
        grid_spec=pltpu.PrefetchScalarGridSpec(
            num_scalar_prefetch=1,
            grid=(12,),
            in_specs=[
                whole(rows, cols, width),
                whole(1, cols, width),
                whole(1, cols, width),
                whole(rows + 2, width),
                whole(rows + 2, width),
                pl.BlockSpec((1, 4, half, width), lambda i, c: kernel_row(i, 1)),
                pl.BlockSpec((1, 4, half, width), lambda i, c: kernel_row(i, 3)),
                tokens_of(hidden),
                tokens_of(hidden),
                pl.BlockSpec(memory_space=pl.ANY),
                pl.BlockSpec(memory_space=pl.ANY),
                pl.BlockSpec(memory_space=pl.ANY),
            ],
            out_specs=[tokens_of(hidden), tokens_of(model), whole(*blocks), whole(*blocks)],
            scratch_shapes=[
                pltpu.VMEM((3, rows + 2, cols, width), BF16),
                pltpu.VMEM((count, model), BF16),
                pltpu.VMEM((count, model), BF16),
                pltpu.VMEM((model, hidden), BF16),
                pltpu.VMEM((count, model), BF16),
                pltpu.VMEM((count, hidden), BF16),
                pltpu.VMEM((count, hidden), BF16),
                pltpu.VMEM((3 * model, count), BF16),
                pltpu.SemaphoreType.DMA((3,)),
            ],
        ),
        out_shape=[
            jax.ShapeDtypeStruct((count, hidden), BF16),
            jax.ShapeDtypeStruct((count, model), BF16),
            jax.ShapeDtypeStruct(blocks, BF16),
            jax.ShapeDtypeStruct(blocks, BF16),
        ],
        compiler_params=params(),
        cost_estimate=cost(18 << 30, 36 << 20),
        name="main",
    )(
        core, lat, before, after, left, right, *[weight.reshape(4, 4, model, width)] * 2,
        h_top, a_top, tokens, cot, w_in,
    )


def tail_body(
    tokens, act, w_out, cot_hbm, before, after, left, right, weight, united, out,
    cot, planes, sem,
):
    step = pl.program_id(0)
    fine_rows, fine_cols, model = cot.shape
    cols = fine_cols // 2
    rows = fine_rows // 2
    copy = pltpu.make_async_copy(cot_hbm, cot, sem.at[0])

    @pl.when(step == 0)
    def _():
        copy.start()

    @pl.when(step < 4)
    def _():
        united[...] = (tokens[...].astype(F32) + dot_nn(act[...], w_out[...])).astype(BF16)

    @pl.when(step == 4)
    def _():
        copy.wait()
        r, c = iota((fine_cols, fine_cols), 0), iota((fine_cols, fine_cols), 1)
        pick = (c == 2 * (r % cols) + r // cols).astype(F32).astype(BF16)
        lefts, rights = left[...].astype(F32), right[...].astype(F32)
        place = iota((cols, model), 0)
        for e in range(fine_rows + 2):
            row = before[0] if e == 0 else after[0] if e == fine_rows + 1 else cot[e - 1]
            found = dot_nn(pick, row)
            even, odd = found[:cols], found[cols:]
            taps = (
                jnp.where(place == 0, lefts[e : e + 1], pltpu.roll(odd, 1, 0)),
                even,
                odd,
                jnp.where(place == cols - 1, rights[e : e + 1], pltpu.roll(even, cols - 1, 0)),
            )
            for tap in range(4):
                planes[e % 2, e // 2, :, tap * model : (tap + 1) * model] = taps[tap].astype(BF16)

    @pl.when(step >= 4)
    def _():
        k = step - 4
        source = planes[k % 2, pl.ds(k // 2, rows)].reshape(rows * cols, 4 * model)
        term = dot_nn(source, weight[0])

        @pl.when(k == 0)
        def _():
            out[...] = term

        @pl.when(k != 0)
        def _():
            out[...] += term


def tail_kernel(tokens, act, w_out, cot, before, after, left, right, weight):
    fine_rows, fine_cols, model = cot.shape
    width = weight.shape[1]
    count, hidden = act.shape
    block = count // 4
    whole = lambda a: pl.BlockSpec(a.shape, lambda i: (0,) * a.ndim)
    size = fine_rows * fine_cols // 4
    tokens_of = lambda w: pl.BlockSpec((block, w), lambda i: (jnp.minimum(i, 3), 0))
    return pl.pallas_call(
        tail_body,
        grid=(8,),
        in_specs=[
            tokens_of(model),
            tokens_of(hidden),
            whole(w_out),
            pl.BlockSpec(memory_space=pl.ANY),
            whole(before),
            whole(after),
            whole(left),
            whole(right),
            pl.BlockSpec((1, 4 * model, width), lambda i: (jnp.maximum(i - 4, 0), 0, 0)),
        ],
        out_specs=[tokens_of(model), pl.BlockSpec((size, width), lambda i: (0, 0))],
        out_shape=[
            jax.ShapeDtypeStruct((count, model), BF16),
            jax.ShapeDtypeStruct((size, width), F32),
        ],
        scratch_shapes=[
            pltpu.VMEM((fine_rows, fine_cols, model), BF16),
            pltpu.VMEM((2, fine_rows // 2 + 1, fine_cols // 2, 4 * model), BF16),
            pltpu.SemaphoreType.DMA((1,)),
        ],
        compiler_params=pltpu.CompilerParams(vmem_limit_bytes=40 << 20),
        cost_estimate=cost(7 << 30, 22 << 20),
        name="tail",
    )(tokens, act, w_out, cot, before, after, left, right, weight.reshape(4, 4 * model, width))


def sum_body(parts, in_grad, out_grad):
    total = parts[0].astype(F32)
    for i in range(1, parts.shape[0]):
        total = total + parts[i].astype(F32)
    in_grad[...] = total[:64]
    packed = total[64:]
    out_grad[...] = jnp.concatenate(
        [packed, pltpu.roll(packed, 64, 1)], axis=0
    ).T[:64, :]


def sum_blocks(parts):
    return pl.pallas_call(
        sum_body,
        out_shape=[
            jax.ShapeDtypeStruct((64, 128), F32),
            jax.ShapeDtypeStruct((64, 64), F32),
        ],
        compiler_params=pltpu.CompilerParams(vmem_limit_bytes=8 << 20),
        cost_estimate=cost(1 << 20, 2 << 20),
        name="sum_blocks",
    )(parts)


def neighbours(array, axis, dim, wrap):
    devices = lax.axis_size(axis)
    up = [(i, (i + 1) % devices) for i in range(devices if wrap else devices - 1)]
    down = [(j, i) for i, j in up]
    length = array.shape[dim]
    last = lax.slice_in_dim(array, length - 1, length, axis=dim)
    first = lax.slice_in_dim(array, 0, 1, axis=dim)
    return lax.ppermute(last, axis, up), lax.ppermute(first, axis, down)


def side_columns(array, before, after):
    devices = lax.axis_size("lon")
    up = [(i, (i + 1) % devices) for i in range(devices)]
    down = [(j, i) for i, j in up]
    column = lambda c: jnp.concatenate([before[:, c], array[:, c], after[:, c]], axis=0)
    return lax.ppermute(column(-1), "lon", up), lax.ppermute(column(0), "lon", down)


def chip_groups():
    return [
        [
            (x * 2 + y_lo) * 16 + z * 4 + y_hi * 2 + core
            for z in range(4)
            for x in range(4)
            for y_hi in range(2)
            for y_lo in range(2)
        ]
        for core in range(2)
    ]


def other_core(array):
    return lax.ppermute(array, "lon", [(i, i ^ 1) for i in range(16)])


def shards(fine_tokens, latents, upsample_weight, uniting_in, uniting_out, cotangent):
    count = fine_tokens.shape[0] * fine_tokens.shape[1]
    model = fine_tokens.shape[2]
    core = (lax.axis_index("lon") % 2).astype(jnp.int32).reshape(1)
    tokens = fine_tokens.reshape(count, model)
    cot = cotangent.reshape(count, model)

    before, after = neighbours(latents, "lat", 0, False)
    left, right = side_columns(latents, before, after)
    a_top = dot_nt(cot, uniting_out).astype(BF16)
    h_top = dot_nn(tokens, uniting_in[:model]).astype(BF16)
    act, up_cot, keep, send = main_kernel(
        core, latents, before, after, left, right, upsample_weight,
        h_top, a_top, tokens, cot, uniting_in,
    )

    up_cot = up_cot.reshape(fine_tokens.shape)
    cot_before, cot_after = neighbours(up_cot, "lat", 0, False)
    other = other_core(send)
    cot_left, cot_right = side_columns(up_cot, cot_before, cot_after)
    halves = (keep.astype(F32) + other.astype(F32)).astype(BF16).reshape(64, 96, 128)
    halves, cot_left, cot_right = lax.optimization_barrier((halves, cot_left, cot_right))
    parts = lax.all_to_all(halves, BOTH, 0, 0, axis_index_groups=chip_groups(), tiled=True)

    united, latent_grad = tail_kernel(
        tokens, act, uniting_out, up_cot, cot_before, cot_after, cot_left, cot_right,
        upsample_weight,
    )
    in_grad, out_grad = sum_blocks(parts)
    return (
        united.reshape(fine_tokens.shape),
        latent_grad.reshape(latents.shape),
        in_grad,
        out_grad,
    )


def solution(mesh):
    return jax.shard_map(
        shards,
        mesh=mesh,
        in_specs=(
            P("lat", "lon", None),
            P("lat", "lon", None),
            P(),
            P(),
            P(),
            P("lat", "lon", None),
        ),
        out_specs=(P("lat", "lon", None), P("lat", "lon", None), P("lon", "lat"), P("lon", "lat")),
        check_vma=False,
    )
```

```python
import jax
import jax.numpy as jnp
from jax import lax
from jax.experimental import pallas as pl
from jax.experimental.pallas import tpu as pltpu
from jax.sharding import PartitionSpec as P

BF16 = jnp.bfloat16
F32 = jnp.float32
BOTH = ("lat", "lon")


def dot_nn(a, b):
    return lax.dot_general(a, b, (((1,), (0,)), ((), ())), preferred_element_type=F32)


def dot_nt(a, b):
    return lax.dot_general(a, b, (((1,), (1,)), ((), ())), preferred_element_type=F32)


def dot_tn(a, b):
    return lax.dot_general(a, b, (((0,), (0,)), ((), ())), preferred_element_type=F32)


def cost(flops, nbytes):
    return pl.CostEstimate(flops=flops, bytes_accessed=nbytes, transcendentals=0)


def params():
    return pltpu.CompilerParams(vmem_limit_bytes=60 << 20)


def iota(shape, dim):
    return lax.broadcasted_iota(jnp.int32, shape, dim)


def main_body(
    core, lat, before, after, left, right, w_a, w_b, tokens_hbm, cot_hbm, w_in_hbm, w_out_hbm,
    act_out, up_cot, keep, send,
    shifts, tokens, cot, w_in, w_out, up, act, pre, turned, sems,
):
    step = pl.program_id(0)
    rows, cols, width = lat.shape
    hidden, model = w_out.shape
    half_model = model // 2
    block = act_out.shape[0]
    copies = [
        pltpu.make_async_copy(source, target, sems.at[i])
        for i, (source, target) in enumerate(
            ((w_in_hbm, w_in), (w_out_hbm, w_out), (tokens_hbm, tokens), (cot_hbm, cot))
        )
    ]

    @pl.when(step == 0)
    def _():
        for copy in copies:
            copy.start()
        lefts, rights = left[...].astype(F32), right[...].astype(F32)
        place = iota((cols, width), 0)
        for r in range(rows + 2):
            row = before[0] if r == 0 else after[0] if r == rows + 1 else lat[r - 1]
            wide = row.astype(F32)
            shifts[1, r] = row
            shifts[0, r] = jnp.where(
                place == 0, lefts[r : r + 1], pltpu.roll(wide, 1, 0)
            ).astype(BF16)
            shifts[2, r] = jnp.where(
                place == cols - 1, rights[r : r + 1], pltpu.roll(wide, cols - 1, 0)
            ).astype(BF16)

    @pl.when(step < 4)
    def _():
        parity, half = step // 2, step % 2
        planes = []
        for taps in (((1, 0), (3, -1)), ((0, 1), (2, 0))):
            total = None
            for weight, start in ((w_a, 1 + parity), (w_b, parity)):
                for tap, move in taps:
                    source = shifts[move + 1, pl.ds(start, rows)].reshape(rows * cols, width)
                    term = dot_nt(source, weight[0, tap])
                    total = term if total is None else total + term
            planes.append(total.astype(BF16))
        size = 2 * cols
        r, k = iota((size, size), 0), iota((size, size), 1)
        spread = (k == (r % 2) * cols + r // 2).astype(F32).astype(BF16)
        for m in range(rows):
            pair = jnp.concatenate([z[m * cols : (m + 1) * cols] for z in planes], axis=0)
            value = dot_nn(spread, pair).astype(BF16)
            up[half, pl.ds(pl.multiple_of((2 * m + parity) * size, size), size)] = value

    @pl.when(step == 4)
    def _():
        for copy in copies:
            copy.wait()

    @pl.when((step >= 4) & (step < 8))
    def _():
        at = pl.ds(pl.multiple_of((step - 4) * block, block), block)
        for n in range(0, hidden, 256):
            span = slice(n, n + 256)
            h = dot_nn(tokens[at, :], w_in[:model, span])
            h += dot_nn(up[0, at], w_in[model : model + half_model, span])
            h += dot_nn(up[1, at], w_in[model + half_model :, span])
            g = 0.5 * jnp.tanh(0.5 * h) + 0.5
            y = h * g
            wide = y.astype(BF16)
            act[at, span] = wide
            act_out[:, span] = wide
            a = dot_nt(cot[at, :], w_out[span, :])
            pre[at, span] = (a * (g + y * (1.0 - g))).astype(BF16)
        up_cot[...] = dot_nt(pre[at, :], w_in[model:, :]).astype(BF16)
        turned[0:model, at] = tokens[at, :].T
        turned[model : model + half_model, at] = up[0, at].T
        turned[model + half_model : 2 * model, at] = up[1, at].T
        turned[2 * model :, at] = cot[at, :].T

    for j in range(4):

        @pl.when(step == 8 + j)
        def _():
            span = slice(j * 256, (j + 1) * 256)
            mine = core[0]
            total = dot_nn(turned[: 2 * model], pre[:, span])
            for z in range(4):
                for y_hi in range(2):
                    base = (z * 2 + y_hi) * 128
                    first, second = total[base : base + 64], total[base + 64 : base + 128]
                    own = jnp.where(mine == 0, first, second).astype(BF16)
                    other = jnp.where(mine == 0, second, first).astype(BF16)
                    for y_lo in range(2):
                        lanes = slice(y_lo * 128, (y_lo + 1) * 128)
                        keep[z, j, y_hi * 2 + y_lo, 0:64] = own[:, lanes]
                        send[z, j, y_hi * 2 + y_lo, 0:64] = other[:, lanes]
            total = dot_nn(turned[2 * model :], act[:, span])
            low = iota((32, 128), 1) < 64
            for lat_id in range(8):
                for y_hi in range(2):
                    lanes = slice(y_hi * 128, (y_hi + 1) * 128)
                    a = total[lat_id * 64 : lat_id * 64 + 32, lanes]
                    b = total[lat_id * 64 + 32 : lat_id * 64 + 64, lanes]
                    first = jnp.where(low, a, pltpu.roll(b, 64, 1))
                    second = jnp.where(low, pltpu.roll(a, 64, 1), b)
                    at = y_hi * 2 + lat_id % 2
                    keep[j, lat_id // 2, at, 64:96] = jnp.where(
                        mine == 0, first, second
                    ).astype(BF16)
                    send[j, lat_id // 2, at, 64:96] = jnp.where(
                        mine == 0, second, first
                    ).astype(BF16)


def main_kernel(core, lat, before, after, left, right, weight, tokens, cot, w_in, w_out):
    rows, cols, width = lat.shape
    model = weight.shape[0] // 16
    half = model // 2
    count = tokens.shape[0]
    hidden = w_out.shape[0]
    block = count // 4
    clamp = lambda i, low: jnp.clip(i - low, 0, 3)
    whole = lambda *shape: pl.BlockSpec(shape, lambda i, c: (0,) * len(shape))
    kernel_row = lambda i, top: (top - clamp(i, 0) // 2, 0, clamp(i, 0) % 2, 0)
    tokens_of = lambda w: pl.BlockSpec((block, w), lambda i, c: (clamp(i, 4), 0))
    blocks = (4, 4, 4, 96, 128)
    return pl.pallas_call(
        main_body,
        grid_spec=pltpu.PrefetchScalarGridSpec(
            num_scalar_prefetch=1,
            grid=(12,),
            in_specs=[
                whole(rows, cols, width),
                whole(1, cols, width),
                whole(1, cols, width),
                whole(rows + 2, width),
                whole(rows + 2, width),
                pl.BlockSpec((1, 4, half, width), lambda i, c: kernel_row(i, 1)),
                pl.BlockSpec((1, 4, half, width), lambda i, c: kernel_row(i, 3)),
                pl.BlockSpec(memory_space=pl.ANY),
                pl.BlockSpec(memory_space=pl.ANY),
                pl.BlockSpec(memory_space=pl.ANY),
                pl.BlockSpec(memory_space=pl.ANY),
            ],
            out_specs=[tokens_of(hidden), tokens_of(model), whole(*blocks), whole(*blocks)],
            scratch_shapes=[
                pltpu.VMEM((3, rows + 2, cols, width), BF16),
                pltpu.VMEM((count, model), BF16),
                pltpu.VMEM((count, model), BF16),
                pltpu.VMEM((2 * model, hidden), BF16),
                pltpu.VMEM((hidden, model), BF16),
                pltpu.VMEM((2, count, half), BF16),
                pltpu.VMEM((count, hidden), BF16),
                pltpu.VMEM((count, hidden), BF16),
                pltpu.VMEM((3 * model, count), BF16),
                pltpu.SemaphoreType.DMA((4,)),
            ],
        ),
        out_shape=[
            jax.ShapeDtypeStruct((count, hidden), BF16),
            jax.ShapeDtypeStruct((count, model), BF16),
            jax.ShapeDtypeStruct(blocks, BF16),
            jax.ShapeDtypeStruct(blocks, BF16),
        ],
        compiler_params=params(),
        cost_estimate=cost(18 << 30, 36 << 20),
        name="main",
    )(
        core, lat, before, after, left, right, *[weight.reshape(4, 4, model, width)] * 2,
        tokens, cot, w_in, w_out,
    )


def tail_body(
    tokens, act, w_out, cot_hbm, before, after, left, right, weight, united, out,
    cot, planes, sem,
):
    step = pl.program_id(0)
    fine_rows, fine_cols, model = cot.shape
    cols = fine_cols // 2
    rows = fine_rows // 2
    copy = pltpu.make_async_copy(cot_hbm, cot, sem.at[0])

    @pl.when(step == 0)
    def _():
        copy.start()

    @pl.when(step < 4)
    def _():
        united[...] = (tokens[...].astype(F32) + dot_nn(act[...], w_out[...])).astype(BF16)

    @pl.when(step == 4)
    def _():
        copy.wait()
        r, c = iota((fine_cols, fine_cols), 0), iota((fine_cols, fine_cols), 1)
        pick = (c == 2 * (r % cols) + r // cols).astype(F32).astype(BF16)
        lefts, rights = left[...].astype(F32), right[...].astype(F32)
        place = iota((cols, model), 0)
        for e in range(fine_rows + 2):
            row = before[0] if e == 0 else after[0] if e == fine_rows + 1 else cot[e - 1]
            found = dot_nn(pick, row)
            even, odd = found[:cols], found[cols:]
            taps = (
                jnp.where(place == 0, lefts[e : e + 1], pltpu.roll(odd, 1, 0)),
                even,
                odd,
                jnp.where(place == cols - 1, rights[e : e + 1], pltpu.roll(even, cols - 1, 0)),
            )
            for tap in range(4):
                planes[e % 2, e // 2, :, tap * model : (tap + 1) * model] = taps[tap].astype(BF16)

    @pl.when(step >= 4)
    def _():
        k = step - 4
        source = planes[k % 2, pl.ds(k // 2, rows)].reshape(rows * cols, 4 * model)
        term = dot_nn(source, weight[0])

        @pl.when(k == 0)
        def _():
            out[...] = term

        @pl.when(k != 0)
        def _():
            out[...] += term


def tail_kernel(tokens, act, w_out, cot, before, after, left, right, weight):
    fine_rows, fine_cols, model = cot.shape
    width = weight.shape[1]
    count, hidden = act.shape
    block = count // 4
    whole = lambda a: pl.BlockSpec(a.shape, lambda i: (0,) * a.ndim)
    size = fine_rows * fine_cols // 4
    tokens_of = lambda w: pl.BlockSpec((block, w), lambda i: (jnp.minimum(i, 3), 0))
    return pl.pallas_call(
        tail_body,
        grid=(8,),
        in_specs=[
            tokens_of(model),
            tokens_of(hidden),
            whole(w_out),
            pl.BlockSpec(memory_space=pl.ANY),
            whole(before),
            whole(after),
            whole(left),
            whole(right),
            pl.BlockSpec((1, 4 * model, width), lambda i: (jnp.maximum(i - 4, 0), 0, 0)),
        ],
        out_specs=[tokens_of(model), pl.BlockSpec((size, width), lambda i: (0, 0))],
        out_shape=[
            jax.ShapeDtypeStruct((count, model), BF16),
            jax.ShapeDtypeStruct((size, width), F32),
        ],
        scratch_shapes=[
            pltpu.VMEM((fine_rows, fine_cols, model), BF16),
            pltpu.VMEM((2, fine_rows // 2 + 1, fine_cols // 2, 4 * model), BF16),
            pltpu.SemaphoreType.DMA((1,)),
        ],
        compiler_params=pltpu.CompilerParams(vmem_limit_bytes=58 << 20),
        cost_estimate=cost(7 << 30, 22 << 20),
        name="tail",
    )(tokens, act, w_out, cot, before, after, left, right, weight.reshape(4, 4 * model, width))


def sum_body(parts, in_grad, out_grad):
    total = parts[0].astype(F32)
    for i in range(1, parts.shape[0]):
        total = total + parts[i].astype(F32)
    in_grad[...] = total[:64]
    packed = total[64:]
    out_grad[...] = jnp.concatenate(
        [packed, pltpu.roll(packed, 64, 1)], axis=0
    ).T[:64, :]


def sum_blocks(parts):
    return pl.pallas_call(
        sum_body,
        out_shape=[
            jax.ShapeDtypeStruct((64, 128), F32),
            jax.ShapeDtypeStruct((64, 64), F32),
        ],
        compiler_params=pltpu.CompilerParams(vmem_limit_bytes=8 << 20),
        cost_estimate=cost(1 << 20, 2 << 20),
        name="sum_blocks",
    )(parts)


def neighbours(array, axis, dim, wrap):
    devices = lax.axis_size(axis)
    up = [(i, (i + 1) % devices) for i in range(devices if wrap else devices - 1)]
    down = [(j, i) for i, j in up]
    length = array.shape[dim]
    last = lax.slice_in_dim(array, length - 1, length, axis=dim)
    first = lax.slice_in_dim(array, 0, 1, axis=dim)
    return lax.ppermute(last, axis, up), lax.ppermute(first, axis, down)


def side_columns(array, before, after):
    devices = lax.axis_size("lon")
    up = [(i, (i + 1) % devices) for i in range(devices)]
    down = [(j, i) for i, j in up]
    column = lambda c: jnp.concatenate([before[:, c], array[:, c], after[:, c]], axis=0)
    return lax.ppermute(column(-1), "lon", up), lax.ppermute(column(0), "lon", down)


def chip_groups():
    return [
        [
            (x * 2 + y_lo) * 16 + z * 4 + y_hi * 2 + core
            for z in range(4)
            for x in range(4)
            for y_hi in range(2)
            for y_lo in range(2)
        ]
        for core in range(2)
    ]


def other_core(array):
    return lax.ppermute(array, "lon", [(i, i ^ 1) for i in range(16)])


def shards(fine_tokens, latents, upsample_weight, uniting_in, uniting_out, cotangent):
    count = fine_tokens.shape[0] * fine_tokens.shape[1]
    model = fine_tokens.shape[2]
    core = (lax.axis_index("lon") % 2).astype(jnp.int32).reshape(1)
    tokens = fine_tokens.reshape(count, model)
    cot = cotangent.reshape(count, model)

    before, after = neighbours(latents, "lat", 0, False)
    left, right = side_columns(latents, before, after)
    act, up_cot, keep, send = main_kernel(
        core, latents, before, after, left, right, upsample_weight,
        tokens, cot, uniting_in, uniting_out,
    )

    up_cot = up_cot.reshape(fine_tokens.shape)
    cot_before, cot_after = neighbours(up_cot, "lat", 0, False)
    other = other_core(send)
    cot_left, cot_right = side_columns(up_cot, cot_before, cot_after)
    halves = (keep.astype(F32) + other.astype(F32)).astype(BF16).reshape(64, 96, 128)
    halves, cot_left, cot_right = lax.optimization_barrier((halves, cot_left, cot_right))
    parts = lax.all_to_all(halves, BOTH, 0, 0, axis_index_groups=chip_groups(), tiled=True)

    united, latent_grad = tail_kernel(
        tokens, act, uniting_out, up_cot, cot_before, cot_after, cot_left, cot_right,
        upsample_weight,
    )
    in_grad, out_grad = sum_blocks(parts)
    return (
        united.reshape(fine_tokens.shape),
        latent_grad.reshape(latents.shape),
        in_grad,
        out_grad,
    )


def solution(mesh):
    return jax.shard_map(
        shards,
        mesh=mesh,
        in_specs=(
            P("lat", "lon", None),
            P("lat", "lon", None),
            P(),
            P(),
            P(),
            P("lat", "lon", None),
        ),
        out_specs=(P("lat", "lon", None), P("lat", "lon", None), P("lon", "lat"), P("lon", "lat")),
        check_vma=False,
    )
```

```python
import jax
import jax.numpy as jnp
from jax import lax
from jax.experimental import pallas as pl
from jax.experimental.pallas import tpu as pltpu
from jax.sharding import PartitionSpec as P

BF16 = jnp.bfloat16
F32 = jnp.float32
BOTH = ("lat", "lon")


def dot_nn(a, b):
    return lax.dot_general(a, b, (((1,), (0,)), ((), ())), preferred_element_type=F32)


def dot_nt(a, b):
    return lax.dot_general(a, b, (((1,), (1,)), ((), ())), preferred_element_type=F32)


def cost(flops, nbytes):
    return pl.CostEstimate(flops=flops, bytes_accessed=nbytes, transcendentals=0)


def params():
    return pltpu.CompilerParams(vmem_limit_bytes=60 << 20)


def iota(shape, dim):
    return lax.broadcasted_iota(jnp.int32, shape, dim)


def main_body(
    core, lat, before, after, left, right, w_a, w_b, tokens_hbm, cot_hbm, w_in_hbm, w_out_hbm,
    act_out, up_cot, up_cot_edge, keep, send,
    sources, edges, tokens, cot, tokens_edge, cot_edge, w_in, w_out, up, act, pre, pre_edge,
    turned, sems,
):
    step = pl.program_id(0)
    rows, cols, width = lat.shape
    hidden, model = w_out.shape
    half_model = model // 2
    block = act_out.shape[0]
    count = tokens.shape[0]
    fine_cols = 2 * cols
    copies = [
        pltpu.make_async_copy(source, target, sems.at[i])
        for i, (source, target) in enumerate(
            ((w_in_hbm, w_in), (w_out_hbm, w_out), (tokens_hbm, tokens), (cot_hbm, cot))
        )
    ]

    @pl.when(step == 0)
    def _():
        for copy in copies:
            copy.start()
        lefts, rights = left[0:16].astype(F32), right[0:16].astype(F32)
        edges[...] = jnp.zeros_like(edges)
        place = iota((cols, width), 0)
        for r in range(rows + 2):
            row = before[0:cols] if r == 0 else after[0:cols] if r == rows + 1 else lat[r - 1]
            wide = row.astype(F32)
            at = slice(16 + r * cols, 16 + (r + 1) * cols)
            sources[0, at] = row
            sources[1, at] = jnp.where(
                place == 0, lefts[r : r + 1], pltpu.roll(wide, 1, 0)
            ).astype(BF16)
            sources[2, at] = jnp.where(
                place == cols - 1, rights[r : r + 1], pltpu.roll(wide, cols - 1, 0)
            ).astype(BF16)
            sources[3, at] = row
            edges[0, r : r + 1] = wide[cols - 1 : cols]
            edges[1, r : r + 1] = wide[0:1]
        last = 16 + (rows + 2) * cols
        for i, edge in enumerate((rights, edges[0], edges[1], lefts)):
            sources[i, 0:16] = edge.astype(BF16)
            sources[i, last : last + 16] = pltpu.roll(edge, 15, 0).astype(BF16)
        for ref, lane, part in ((tokens_edge, cols, 16), (cot_edge, cols + fine_cols, 48)):
            ref[0:fine_cols] = before[lane : lane + fine_cols]
            ref[fine_cols : 2 * fine_cols] = after[lane : lane + fine_cols]
            ref[2 * fine_cols : 2 * fine_cols + 32] = left[part : part + 32]
            ref[2 * fine_cols + 32 :] = right[part : part + 32]

    @pl.when(step < 4)
    def _():
        parity, half = step // 2, step % 2
        size = (rows + 1) * cols
        planes = []
        for q, taps in enumerate((((1, 0), (3, 1)), ((0, 2), (2, 3)))):
            total_a = total_b = None
            for tap, i in taps:
                term_a = dot_nt(sources[i, 16 + cols : 32 + cols + size], w_a[0, tap])
                term_b = dot_nt(sources[i, 0 : 16 + size], w_b[0, tap])
                total_a = term_a if total_a is None else total_a + term_a
                total_b = term_b if total_b is None else total_b + term_b
            planes.append((total_a[:size] + total_b[16:]).astype(BF16))
            side = (total_a[size:] + total_b[:16]).astype(BF16)
            at = count + 2 * fine_cols + (1 - q) * 32 + (1 - parity) * 16
            up[half, pl.ds(pl.multiple_of(at, 16), 16)] = side
        r, k = iota((fine_cols, fine_cols), 0), iota((fine_cols, fine_cols), 1)
        spread = (k == (r % 2) * cols + r // 2).astype(F32).astype(BF16)
        for m in range(rows + 1):
            pair = jnp.concatenate([z[m * cols : (m + 1) * cols] for z in planes], axis=0)
            value = dot_nn(spread, pair).astype(BF16)
            even = 2 * m * fine_cols if m < rows else count + fine_cols
            odd = (2 * m - 1) * fine_cols if m > 0 else count
            at = even + parity * (odd - even)
            up[half, pl.ds(pl.multiple_of(at, 128), fine_cols)] = value

    @pl.when(step == 4)
    def _():
        for copy in copies:
            copy.wait()

    def network(tokens_of, up_of, cot_of, span):
        h = dot_nn(tokens_of(), w_in[:model, span])
        h += dot_nn(up_of(0), w_in[model : model + half_model, span])
        h += dot_nn(up_of(1), w_in[model + half_model :, span])
        g = 0.5 * jnp.tanh(0.5 * h) + 0.5
        y = h * g
        a = dot_nt(cot_of(), w_out[span, :])
        return y.astype(BF16), (a * (g + y * (1.0 - g))).astype(BF16)

    @pl.when(step == 4)
    def _():
        for n in range(0, hidden, 256):
            span = slice(n, n + 256)
            _, pre_edge[:, span] = network(
                lambda: tokens_edge[...], lambda i: up[i, count:], lambda: cot_edge[...], span
            )
        up_cot_edge[...] = dot_nt(pre_edge[...], w_in[model:, :]).astype(BF16)

    @pl.when((step > 4) & (step < 9))
    def _():
        at = pl.ds(pl.multiple_of((step - 5) * block, block), block)
        for n in range(0, hidden, 256):
            span = slice(n, n + 256)
            wide, grad = network(
                lambda: tokens[at, :], lambda i: up[i, at], lambda: cot[at, :], span
            )
            act[at, span] = wide
            act_out[:, span] = wide
            pre[at, span] = grad
        up_cot[...] = dot_nt(pre[at, :], w_in[model:, :]).astype(BF16)
        turned[0:model, at] = tokens[at, :].T
        turned[model : model + half_model, at] = up[0, at].T
        turned[model + half_model : 2 * model, at] = up[1, at].T
        turned[2 * model :, at] = cot[at, :].T

    for j in range(4):

        @pl.when(step == 9 + j)
        def _():
            span = slice(j * 256, (j + 1) * 256)
            mine = core[0]
            total = dot_nn(turned[: 2 * model], pre[:, span])
            for z in range(4):
                for y_hi in range(2):
                    base = (z * 2 + y_hi) * 128
                    first, second = total[base : base + 64], total[base + 64 : base + 128]
                    own = jnp.where(mine == 0, first, second).astype(BF16)
                    other = jnp.where(mine == 0, second, first).astype(BF16)
                    for y_lo in range(2):
                        lanes = slice(y_lo * 128, (y_lo + 1) * 128)
                        keep[z, j, y_hi * 2 + y_lo, 0:64] = own[:, lanes]
                        send[z, j, y_hi * 2 + y_lo, 0:64] = other[:, lanes]
            total = dot_nn(turned[2 * model :], act[:, span])
            low = iota((32, 128), 1) < 64
            for lat_id in range(8):
                for y_hi in range(2):
                    lanes = slice(y_hi * 128, (y_hi + 1) * 128)
                    a = total[lat_id * 64 : lat_id * 64 + 32, lanes]
                    b = total[lat_id * 64 + 32 : lat_id * 64 + 64, lanes]
                    first = jnp.where(low, a, pltpu.roll(b, 64, 1))
                    second = jnp.where(low, pltpu.roll(a, 64, 1), b)
                    at = y_hi * 2 + lat_id % 2
                    keep[j, lat_id // 2, at, 64:96] = jnp.where(
                        mine == 0, first, second
                    ).astype(BF16)
                    send[j, lat_id // 2, at, 64:96] = jnp.where(
                        mine == 0, second, first
                    ).astype(BF16)


def main_kernel(core, lat, before, after, left, right, weight, tokens, cot, w_in, w_out):
    rows, cols, width = lat.shape
    model = weight.shape[0] // 16
    half = model // 2
    count = tokens.shape[0]
    hidden = w_out.shape[0]
    block = count // 4
    edge = 4 * cols + 64
    clamp = lambda i, low: jnp.clip(i - low, 0, 3)
    whole = lambda *shape: pl.BlockSpec(shape, lambda i, c: (0,) * len(shape))
    kernel_row = lambda i, top: (top - clamp(i, 0) // 2, 0, clamp(i, 0) % 2, 0)
    tokens_of = lambda w: pl.BlockSpec((block, w), lambda i, c: (clamp(i, 5), 0))
    blocks = (4, 4, 4, 96, 128)
    return pl.pallas_call(
        main_body,
        grid_spec=pltpu.PrefetchScalarGridSpec(
            num_scalar_prefetch=1,
            grid=(13,),
            in_specs=[
                whole(rows, cols, width),
                whole(*before.shape),
                whole(*after.shape),
                whole(*left.shape),
                whole(*right.shape),
                pl.BlockSpec((1, 4, half, width), lambda i, c: kernel_row(i, 1)),
                pl.BlockSpec((1, 4, half, width), lambda i, c: kernel_row(i, 3)),
                pl.BlockSpec(memory_space=pl.ANY),
                pl.BlockSpec(memory_space=pl.ANY),
                pl.BlockSpec(memory_space=pl.ANY),
                pl.BlockSpec(memory_space=pl.ANY),
            ],
            out_specs=[
                tokens_of(hidden),
                tokens_of(model),
                whole(edge, model),
                whole(*blocks),
                whole(*blocks),
            ],
            scratch_shapes=[
                pltpu.VMEM((4, (rows + 2) * cols + 32, width), BF16),
                pltpu.VMEM((2, 16, width), F32),
                pltpu.VMEM((count, model), BF16),
                pltpu.VMEM((count, model), BF16),
                pltpu.VMEM((edge, model), BF16),
                pltpu.VMEM((edge, model), BF16),
                pltpu.VMEM((2 * model, hidden), BF16),
                pltpu.VMEM((hidden, model), BF16),
                pltpu.VMEM((2, count + edge, half), BF16),
                pltpu.VMEM((count, hidden), BF16),
                pltpu.VMEM((count, hidden), BF16),
                pltpu.VMEM((edge, hidden), BF16),
                pltpu.VMEM((3 * model, count), BF16),
                pltpu.SemaphoreType.DMA((4,)),
            ],
        ),
        out_shape=[
            jax.ShapeDtypeStruct((count, hidden), BF16),
            jax.ShapeDtypeStruct((count, model), BF16),
            jax.ShapeDtypeStruct((edge, model), BF16),
            jax.ShapeDtypeStruct(blocks, BF16),
            jax.ShapeDtypeStruct(blocks, BF16),
        ],
        compiler_params=params(),
        cost_estimate=cost(20 << 30, 36 << 20),
        name="main",
    )(
        core, lat, before, after, left, right, *[weight.reshape(4, 4, model, width)] * 2,
        tokens, cot, w_in, w_out,
    )


def tail_body(
    tokens, act, w_out, cot_hbm, edge, weight, united, out,
    cot, planes, sem,
):
    step = pl.program_id(0)
    fine_rows, fine_cols, model = cot.shape
    cols = fine_cols // 2
    rows = fine_rows // 2
    copy = pltpu.make_async_copy(cot_hbm, cot, sem.at[0])

    @pl.when(step == 0)
    def _():
        copy.start()

    @pl.when(step < 4)
    def _():
        united[...] = (tokens[...].astype(F32) + dot_nn(act[...], w_out[...])).astype(BF16)

    @pl.when(step == 4)
    def _():
        copy.wait()
        r, c = iota((fine_cols, fine_cols), 0), iota((fine_cols, fine_cols), 1)
        pick = (c == 2 * (r % cols) + r // cols).astype(F32).astype(BF16)
        lefts, rights = [
            edge[2 * fine_cols + i : 2 * fine_cols + i + 32].astype(F32) for i in (0, 32)
        ]
        place = iota((cols, model), 0)
        for e in range(fine_rows + 2):
            if e == 0:
                row = edge[0:fine_cols]
            elif e == fine_rows + 1:
                row = edge[fine_cols : 2 * fine_cols]
            else:
                row = cot[e - 1]
            at = e // 2 + 16 * (e % 2)
            found = dot_nn(pick, row)
            even, odd = found[:cols], found[cols:]
            taps = (
                jnp.where(place == 0, lefts[at : at + 1], pltpu.roll(odd, 1, 0)),
                even,
                odd,
                jnp.where(place == cols - 1, rights[at : at + 1], pltpu.roll(even, cols - 1, 0)),
            )
            for tap in range(4):
                planes[e % 2, e // 2, :, tap * model : (tap + 1) * model] = taps[tap].astype(BF16)

    @pl.when(step >= 4)
    def _():
        k = step - 4
        source = planes[k % 2, pl.ds(k // 2, rows)].reshape(rows * cols, 4 * model)
        term = dot_nn(source, weight[0])

        @pl.when(k == 0)
        def _():
            out[...] = term

        @pl.when(k != 0)
        def _():
            out[...] += term


def tail_kernel(tokens, act, w_out, cot, edge, weight):
    fine_rows, fine_cols, model = cot.shape
    width = weight.shape[1]
    count, hidden = act.shape
    block = count // 4
    whole = lambda a: pl.BlockSpec(a.shape, lambda i: (0,) * a.ndim)
    size = fine_rows * fine_cols // 4
    tokens_of = lambda w: pl.BlockSpec((block, w), lambda i: (jnp.minimum(i, 3), 0))
    return pl.pallas_call(
        tail_body,
        grid=(8,),
        in_specs=[
            tokens_of(model),
            tokens_of(hidden),
            whole(w_out),
            pl.BlockSpec(memory_space=pl.ANY),
            whole(edge),
            pl.BlockSpec((1, 4 * model, width), lambda i: (jnp.maximum(i - 4, 0), 0, 0)),
        ],
        out_specs=[tokens_of(model), pl.BlockSpec((size, width), lambda i: (0, 0))],
        out_shape=[
            jax.ShapeDtypeStruct((count, model), BF16),
            jax.ShapeDtypeStruct((size, width), F32),
        ],
        scratch_shapes=[
            pltpu.VMEM((fine_rows, fine_cols, model), BF16),
            pltpu.VMEM((2, fine_rows // 2 + 1, fine_cols // 2, 4 * model), BF16),
            pltpu.SemaphoreType.DMA((1,)),
        ],
        compiler_params=pltpu.CompilerParams(vmem_limit_bytes=58 << 20),
        cost_estimate=cost(7 << 30, 22 << 20),
        name="tail",
    )(tokens, act, w_out, cot, edge, weight.reshape(4, 4 * model, width))


def sum_body(parts, in_grad, out_grad):
    total = parts[0].astype(F32)
    for i in range(1, parts.shape[0]):
        total = total + parts[i].astype(F32)
    in_grad[...] = total[:64]
    packed = total[64:]
    out_grad[...] = jnp.concatenate(
        [packed, pltpu.roll(packed, 64, 1)], axis=0
    ).T[:64, :]


def sum_blocks(parts):
    return pl.pallas_call(
        sum_body,
        out_shape=[
            jax.ShapeDtypeStruct((64, 128), F32),
            jax.ShapeDtypeStruct((64, 64), F32),
        ],
        compiler_params=pltpu.CompilerParams(vmem_limit_bytes=8 << 20),
        cost_estimate=cost(1 << 20, 2 << 20),
        name="sum_blocks",
    )(parts)


def swap(last, first, axis, wrap):
    devices = lax.axis_size(axis)
    up = [(i, (i + 1) % devices) for i in range(devices if wrap else devices - 1)]
    down = [(j, i) for i, j in up]
    return lax.ppermute(last, axis, up), lax.ppermute(first, axis, down)


def halos(latents, tokens, cot):
    cols, fine_cols = latents.shape[1], tokens.shape[1]
    row = lambda i: jnp.concatenate([latents[i], tokens[i], cot[i]], axis=0)
    before, after = swap(row(-1), row(0), "lat", False)

    def column(c):
        parts = []
        place = c % cols
        pad = lambda a: jnp.pad(a, ((0, 16 - a.shape[0]), (0, 0)))
        ends = [a[place : place + 1] for a in (before, after)]
        parts.append(pad(jnp.concatenate([ends[0], latents[:, c], ends[1]], axis=0)))
        for fine, start in ((tokens, cols), (cot, cols + fine_cols)):
            place = start + c % fine_cols
            ends = [a[place : place + 1] for a in (before, after)]
            parts.append(pad(jnp.concatenate([ends[0], fine[1::2, c]], axis=0)))
            parts.append(pad(jnp.concatenate([fine[0::2, c], ends[1]], axis=0)))
        return jnp.concatenate(parts, axis=0)

    left, right = swap(column(-1), column(0), "lon", True)
    return before, after, left, right


def chip_groups():
    return [
        [
            (x * 2 + y_lo) * 16 + z * 4 + y_hi * 2 + core
            for z in range(4)
            for x in range(4)
            for y_hi in range(2)
            for y_lo in range(2)
        ]
        for core in range(2)
    ]


def other_core(array):
    return lax.ppermute(array, "lon", [(i, i ^ 1) for i in range(16)])


def shards(fine_tokens, latents, upsample_weight, uniting_in, uniting_out, cotangent):
    count = fine_tokens.shape[0] * fine_tokens.shape[1]
    model = fine_tokens.shape[2]
    core = (lax.axis_index("lon") % 2).astype(jnp.int32).reshape(1)
    tokens = fine_tokens.reshape(count, model)
    cot = cotangent.reshape(count, model)

    before, after, left, right = halos(latents, fine_tokens, cotangent)
    act, up_cot, up_cot_edge, keep, send = main_kernel(
        core, latents, before, after, left, right, upsample_weight,
        tokens, cot, uniting_in, uniting_out,
    )
    other = other_core(send)
    halves = (keep.astype(F32) + other.astype(F32)).astype(BF16).reshape(64, 96, 128)
    parts = lax.all_to_all(
        halves, BOTH, 0, 0, axis_index_groups=chip_groups(), tiled=True
    )
    united, latent_grad = tail_kernel(
        tokens, act, uniting_out, up_cot.reshape(fine_tokens.shape), up_cot_edge,
        upsample_weight,
    )
    in_grad, out_grad = sum_blocks(parts)
    return (
        united.reshape(fine_tokens.shape),
        latent_grad.reshape(latents.shape),
        in_grad,
        out_grad,
    )


def solution(mesh):
    return jax.shard_map(
        shards,
        mesh=mesh,
        in_specs=(
            P("lat", "lon", None),
            P("lat", "lon", None),
            P(),
            P(),
            P(),
            P("lat", "lon", None),
        ),
        out_specs=(P("lat", "lon", None), P("lat", "lon", None), P("lon", "lat"), P("lon", "lat")),
        check_vma=False,
    )
```

```python
import jax
import jax.numpy as jnp
from jax import lax
from jax.experimental import pallas as pl
from jax.experimental.pallas import tpu as pltpu
from jax.sharding import PartitionSpec as P

BF16 = jnp.bfloat16
F32 = jnp.float32
BOTH = ("lat", "lon")


def dot_nn(a, b):
    return lax.dot_general(a, b, (((1,), (0,)), ((), ())), preferred_element_type=F32)


def dot_nt(a, b):
    return lax.dot_general(a, b, (((1,), (1,)), ((), ())), preferred_element_type=F32)


def cost(flops, nbytes):
    return pl.CostEstimate(flops=flops, bytes_accessed=nbytes, transcendentals=0)


def params():
    return pltpu.CompilerParams(vmem_limit_bytes=60 << 20)


def iota(shape, dim):
    return lax.broadcasted_iota(jnp.int32, shape, dim)


def main_body(
    core, lat, before, after, left, right, w_a, w_b, tokens_hbm, cot_hbm, w_in_hbm, w_out_hbm,
    act_out, up_cot, up_cot_edge, first_row, last_row, keep, send,
    sources, edges, tokens, cot, tokens_edge, cot_edge, w_in, w_out, up, act, pre, pre_edge,
    turned, sems,
):
    step = pl.program_id(0)
    rows, cols, width = lat.shape
    hidden, model = w_out.shape
    half_model = model // 2
    block = act_out.shape[0]
    count = tokens.shape[0]
    fine_cols = 2 * cols
    copies = [
        pltpu.make_async_copy(source, target, sems.at[i])
        for i, (source, target) in enumerate(
            ((w_in_hbm, w_in), (w_out_hbm, w_out), (tokens_hbm, tokens), (cot_hbm, cot))
        )
    ]

    @pl.when(step == 0)
    def _():
        for copy in copies:
            copy.start()
        lefts, rights = left[0:16].astype(F32), right[0:16].astype(F32)
        edges[...] = jnp.zeros_like(edges)
        place = iota((cols, width), 0)
        for r in range(rows + 2):
            row = before[0:cols] if r == 0 else after[0:cols] if r == rows + 1 else lat[r - 1]
            wide = row.astype(F32)
            at = slice(16 + r * cols, 16 + (r + 1) * cols)
            sources[0, at] = row
            sources[1, at] = jnp.where(
                place == 0, lefts[r : r + 1], pltpu.roll(wide, 1, 0)
            ).astype(BF16)
            sources[2, at] = jnp.where(
                place == cols - 1, rights[r : r + 1], pltpu.roll(wide, cols - 1, 0)
            ).astype(BF16)
            sources[3, at] = row
            edges[0, r : r + 1] = wide[cols - 1 : cols]
            edges[1, r : r + 1] = wide[0:1]
        last = 16 + (rows + 2) * cols
        for i, edge in enumerate((rights, edges[0], edges[1], lefts)):
            sources[i, 0:16] = edge.astype(BF16)
            sources[i, last : last + 16] = pltpu.roll(edge, 15, 0).astype(BF16)
        for ref, part in ((tokens_edge, 16), (cot_edge, 48)):
            ref[0:32] = left[part : part + 32]
            ref[32:] = right[part : part + 32]

    @pl.when(step < 4)
    def _():
        parity, half = step // 2, step % 2
        size = (rows + 1) * cols
        planes = []
        for q, taps in enumerate((((1, 0), (3, 1)), ((0, 2), (2, 3)))):
            total_a = total_b = None
            for tap, i in taps:
                term_a = dot_nt(sources[i, 16 + cols : 32 + cols + size], w_a[0, tap])
                term_b = dot_nt(sources[i, 0 : 16 + size], w_b[0, tap])
                total_a = term_a if total_a is None else total_a + term_a
                total_b = term_b if total_b is None else total_b + term_b
            planes.append((total_a[:size] + total_b[16:]).astype(BF16))
            side = (total_a[size:] + total_b[:16]).astype(BF16)
            at = count + fine_cols + (1 - q) * 32 + (1 - parity) * 16
            up[half, pl.ds(pl.multiple_of(at, 16), 16)] = side
        r, k = iota((fine_cols, fine_cols), 0), iota((fine_cols, fine_cols), 1)
        spread = (k == (r % 2) * cols + r // 2).astype(F32).astype(BF16)
        for m in range(rows + 1):
            pair = jnp.concatenate([z[m * cols : (m + 1) * cols] for z in planes], axis=0)
            value = dot_nn(spread, pair).astype(BF16)
            even = 2 * m * fine_cols if m < rows else count
            odd = (2 * m - 1) * fine_cols if m > 0 else count
            at = even + parity * (odd - even)
            up[half, pl.ds(pl.multiple_of(at, 128), fine_cols)] = value

    @pl.when(step == 4)
    def _():
        for copy in copies:
            copy.wait()

    def network(tokens_of, up_of, cot_of, span):
        h = dot_nn(tokens_of(), w_in[:model, span])
        h += dot_nn(up_of(0), w_in[model : model + half_model, span])
        h += dot_nn(up_of(1), w_in[model + half_model :, span])
        g = 0.5 * jnp.tanh(0.5 * h) + 0.5
        y = h * g
        a = dot_nt(cot_of(), w_out[span, :])
        return y.astype(BF16), (a * (g + y * (1.0 - g))).astype(BF16)

    @pl.when(step == 4)
    def _():
        for n in range(0, hidden, 256):
            span = slice(n, n + 256)
            _, pre_edge[:, span] = network(
                lambda: tokens_edge[...], lambda i: up[i, count + fine_cols :], lambda: cot_edge[...], span
            )
        value = dot_nt(pre_edge[...], w_in[model:, :]).astype(BF16)
        up_cot_edge[...] = value
        for i in range(2):
            at = slice(fine_cols + 16 * i, fine_cols + 16 * i + 16)
            last_row[at] = value[32 * i : 32 * i + 16]
            first_row[at] = value[32 * i + 16 : 32 * i + 32]

    @pl.when((step > 4) & (step < 9))
    def _():
        at = pl.ds(pl.multiple_of((step - 5) * block, block), block)
        for n in range(0, hidden, 256):
            span = slice(n, n + 256)
            wide, grad = network(
                lambda: tokens[at, :], lambda i: up[i, at], lambda: cot[at, :], span
            )
            act[at, span] = wide
            act_out[:, span] = wide
            pre[at, span] = grad
        value = dot_nt(pre[at, :], w_in[model:, :]).astype(BF16)
        up_cot[...] = value

        @pl.when(step == 5)
        def _():
            first_row[0:fine_cols] = value[:fine_cols]

        @pl.when(step == 8)
        def _():
            last_row[0:fine_cols] = value[block - fine_cols :]

        turned[0:model, at] = tokens[at, :].T
        turned[model : model + half_model, at] = up[0, at].T
        turned[model + half_model : 2 * model, at] = up[1, at].T
        turned[2 * model :, at] = cot[at, :].T

    for j in range(4):

        @pl.when(step == 9 + j)
        def _():
            span = slice(j * 256, (j + 1) * 256)
            mine = core[0]
            total = dot_nn(turned[: 2 * model], pre[:, span])
            for z in range(4):
                for y_hi in range(2):
                    base = (z * 2 + y_hi) * 128
                    first, second = total[base : base + 64], total[base + 64 : base + 128]
                    own = jnp.where(mine == 0, first, second).astype(BF16)
                    other = jnp.where(mine == 0, second, first).astype(BF16)
                    for y_lo in range(2):
                        lanes = slice(y_lo * 128, (y_lo + 1) * 128)
                        keep[z, j, y_hi * 2 + y_lo, 0:64] = own[:, lanes]
                        send[z, j, y_hi * 2 + y_lo, 0:64] = other[:, lanes]
            total = dot_nn(turned[2 * model :], act[:, span])
            low = iota((32, 128), 1) < 64
            for lat_id in range(8):
                for y_hi in range(2):
                    lanes = slice(y_hi * 128, (y_hi + 1) * 128)
                    a = total[lat_id * 64 : lat_id * 64 + 32, lanes]
                    b = total[lat_id * 64 + 32 : lat_id * 64 + 64, lanes]
                    first = jnp.where(low, a, pltpu.roll(b, 64, 1))
                    second = jnp.where(low, pltpu.roll(a, 64, 1), b)
                    at = y_hi * 2 + lat_id % 2
                    keep[j, lat_id // 2, at, 64:96] = jnp.where(
                        mine == 0, first, second
                    ).astype(BF16)
                    send[j, lat_id // 2, at, 64:96] = jnp.where(
                        mine == 0, second, first
                    ).astype(BF16)


def main_kernel(core, lat, before, after, left, right, weight, tokens, cot, w_in, w_out):
    rows, cols, width = lat.shape
    model = weight.shape[0] // 16
    half = model // 2
    count = tokens.shape[0]
    hidden = w_out.shape[0]
    block = count // 4
    edge = 64
    pack = 2 * cols + 32
    clamp = lambda i, low: jnp.clip(i - low, 0, 3)
    whole = lambda *shape: pl.BlockSpec(shape, lambda i, c: (0,) * len(shape))
    kernel_row = lambda i, top: (top - clamp(i, 0) // 2, 0, clamp(i, 0) % 2, 0)
    tokens_of = lambda w: pl.BlockSpec((block, w), lambda i, c: (clamp(i, 5), 0))
    blocks = (4, 4, 4, 96, 128)
    return pl.pallas_call(
        main_body,
        grid_spec=pltpu.PrefetchScalarGridSpec(
            num_scalar_prefetch=1,
            grid=(13,),
            in_specs=[
                whole(rows, cols, width),
                whole(*before.shape),
                whole(*after.shape),
                whole(*left.shape),
                whole(*right.shape),
                pl.BlockSpec((1, 4, half, width), lambda i, c: kernel_row(i, 1)),
                pl.BlockSpec((1, 4, half, width), lambda i, c: kernel_row(i, 3)),
                pl.BlockSpec(memory_space=pl.ANY),
                pl.BlockSpec(memory_space=pl.ANY),
                pl.BlockSpec(memory_space=pl.ANY),
                pl.BlockSpec(memory_space=pl.ANY),
            ],
            out_specs=[
                tokens_of(hidden),
                tokens_of(model),
                whole(edge, model),
                whole(pack, model),
                whole(pack, model),
                whole(*blocks),
                whole(*blocks),
            ],
            scratch_shapes=[
                pltpu.VMEM((4, (rows + 2) * cols + 32, width), BF16),
                pltpu.VMEM((2, 16, width), F32),
                pltpu.VMEM((count, model), BF16),
                pltpu.VMEM((count, model), BF16),
                pltpu.VMEM((edge, model), BF16),
                pltpu.VMEM((edge, model), BF16),
                pltpu.VMEM((2 * model, hidden), BF16),
                pltpu.VMEM((hidden, model), BF16),
                pltpu.VMEM((2, count + 2 * cols + edge, half), BF16),
                pltpu.VMEM((count, hidden), BF16),
                pltpu.VMEM((count, hidden), BF16),
                pltpu.VMEM((edge, hidden), BF16),
                pltpu.VMEM((3 * model, count), BF16),
                pltpu.SemaphoreType.DMA((4,)),
            ],
        ),
        out_shape=[
            jax.ShapeDtypeStruct((count, hidden), BF16),
            jax.ShapeDtypeStruct((count, model), BF16),
            jax.ShapeDtypeStruct((edge, model), BF16),
            jax.ShapeDtypeStruct((pack, model), BF16),
            jax.ShapeDtypeStruct((pack, model), BF16),
            jax.ShapeDtypeStruct(blocks, BF16),
            jax.ShapeDtypeStruct(blocks, BF16),
        ],
        compiler_params=params(),
        cost_estimate=cost(20 << 30, 36 << 20),
        name="main",
    )(
        core, lat, before, after, left, right, *[weight.reshape(4, 4, model, width)] * 2,
        tokens, cot, w_in, w_out,
    )


def tail_body(
    tokens, act, w_out, cot_hbm, edge, before, after, weight, united, out,
    cot, planes, sem,
):
    step = pl.program_id(0)
    fine_rows, fine_cols, model = cot.shape
    cols = fine_cols // 2
    rows = fine_rows // 2
    copy = pltpu.make_async_copy(cot_hbm, cot, sem.at[0])

    @pl.when(step == 0)
    def _():
        copy.start()

    @pl.when(step < 4)
    def _():
        united[...] = (tokens[...].astype(F32) + dot_nn(act[...], w_out[...])).astype(BF16)

    @pl.when(step == 4)
    def _():
        copy.wait()
        r, c = iota((fine_cols, fine_cols), 0), iota((fine_cols, fine_cols), 1)
        pick = (c == 2 * (r % cols) + r // cols).astype(F32).astype(BF16)
        sides, above, below = [ref.astype(F32) for ref in (
            edge[...], before[fine_cols:], after[fine_cols:]
        )]
        place = iota((cols, model), 0)
        for e in range(fine_rows + 2):
            if e == 0:
                row, left, right = before[0:fine_cols], above[8:9], above[24:25]
            elif e == fine_rows + 1:
                row, left, right = after[0:fine_cols], below[0:1], below[16:17]
            else:
                at = e // 2 + 16 * (e % 2)
                row, left, right = cot[e - 1], sides[at : at + 1], sides[at + 32 : at + 33]
            found = dot_nn(pick, row)
            even, odd = found[:cols], found[cols:]
            taps = (
                jnp.where(place == 0, left, pltpu.roll(odd, 1, 0)),
                even,
                odd,
                jnp.where(place == cols - 1, right, pltpu.roll(even, cols - 1, 0)),
            )
            for tap in range(4):
                planes[e % 2, e // 2, :, tap * model : (tap + 1) * model] = taps[tap].astype(BF16)

    @pl.when(step >= 4)
    def _():
        k = step - 4
        source = planes[k % 2, pl.ds(k // 2, rows)].reshape(rows * cols, 4 * model)
        term = dot_nn(source, weight[0])

        @pl.when(k == 0)
        def _():
            out[...] = term

        @pl.when(k != 0)
        def _():
            out[...] += term


def tail_kernel(tokens, act, w_out, cot, edge, before, after, weight):
    fine_rows, fine_cols, model = cot.shape
    width = weight.shape[1]
    count, hidden = act.shape
    block = count // 4
    whole = lambda a: pl.BlockSpec(a.shape, lambda i: (0,) * a.ndim)
    size = fine_rows * fine_cols // 4
    tokens_of = lambda w: pl.BlockSpec((block, w), lambda i: (jnp.minimum(i, 3), 0))
    return pl.pallas_call(
        tail_body,
        grid=(8,),
        in_specs=[
            tokens_of(model),
            tokens_of(hidden),
            whole(w_out),
            pl.BlockSpec(memory_space=pl.ANY),
            whole(edge),
            whole(before),
            whole(after),
            pl.BlockSpec((1, 4 * model, width), lambda i: (jnp.maximum(i - 4, 0), 0, 0)),
        ],
        out_specs=[tokens_of(model), pl.BlockSpec((size, width), lambda i: (0, 0))],
        out_shape=[
            jax.ShapeDtypeStruct((count, model), BF16),
            jax.ShapeDtypeStruct((size, width), F32),
        ],
        scratch_shapes=[
            pltpu.VMEM((fine_rows, fine_cols, model), BF16),
            pltpu.VMEM((2, fine_rows // 2 + 1, fine_cols // 2, 4 * model), BF16),
            pltpu.SemaphoreType.DMA((1,)),
        ],
        compiler_params=pltpu.CompilerParams(vmem_limit_bytes=58 << 20),
        cost_estimate=cost(7 << 30, 22 << 20),
        name="tail",
    )(tokens, act, w_out, cot, edge, before, after, weight.reshape(4, 4 * model, width))


def sum_body(parts, in_grad, out_grad):
    total = parts[0].astype(F32)
    for i in range(1, parts.shape[0]):
        total = total + parts[i].astype(F32)
    in_grad[...] = total[:64]
    packed = total[64:]
    out_grad[...] = jnp.concatenate(
        [packed, pltpu.roll(packed, 64, 1)], axis=0
    ).T[:64, :]


def sum_blocks(parts):
    return pl.pallas_call(
        sum_body,
        out_shape=[
            jax.ShapeDtypeStruct((64, 128), F32),
            jax.ShapeDtypeStruct((64, 64), F32),
        ],
        compiler_params=pltpu.CompilerParams(vmem_limit_bytes=8 << 20),
        cost_estimate=cost(1 << 20, 2 << 20),
        name="sum_blocks",
    )(parts)


def swap(last, first, axis, wrap):
    devices = lax.axis_size(axis)
    up = [(i, (i + 1) % devices) for i in range(devices if wrap else devices - 1)]
    down = [(j, i) for i, j in up]
    return lax.ppermute(last, axis, up), lax.ppermute(first, axis, down)


def halos(latents, tokens, cot):
    before, after = swap(latents[-1], latents[0], "lat", False)

    def column(c):
        place = c % latents.shape[1]
        ends = [a[place : place + 1] for a in (before, after)]
        parts = [ends[0], latents[:, c], ends[1], jnp.zeros((6, latents.shape[2]), BF16)]
        for fine in (tokens, cot):
            parts.append(jnp.pad(fine[1::2, c], ((1, 7), (0, 0))))
            parts.append(jnp.pad(fine[0::2, c], ((0, 8), (0, 0))))
        return jnp.concatenate(parts, axis=0)

    left, right = swap(column(-1), column(0), "lon", True)
    return before, after, left, right


def chip_groups():
    return [
        [
            (x * 2 + y_lo) * 16 + z * 4 + y_hi * 2 + core
            for z in range(4)
            for x in range(4)
            for y_hi in range(2)
            for y_lo in range(2)
        ]
        for core in range(2)
    ]


def other_core(array):
    return lax.ppermute(array, "lon", [(i, i ^ 1) for i in range(16)])


def shards(fine_tokens, latents, upsample_weight, uniting_in, uniting_out, cotangent):
    count = fine_tokens.shape[0] * fine_tokens.shape[1]
    model = fine_tokens.shape[2]
    core = (lax.axis_index("lon") % 2).astype(jnp.int32).reshape(1)
    tokens = fine_tokens.reshape(count, model)
    cot = cotangent.reshape(count, model)

    before, after, left, right = halos(latents, fine_tokens, cotangent)
    act, up_cot, up_cot_edge, first_row, last_row, keep, send = main_kernel(
        core, latents, before, after, left, right, upsample_weight,
        tokens, cot, uniting_in, uniting_out,
    )
    other = other_core(send)
    above, below = swap(last_row, first_row, "lat", False)
    halves = (keep.astype(F32) + other.astype(F32)).astype(BF16).reshape(64, 96, 128)
    halves, above, below = lax.optimization_barrier((halves, above, below))
    parts = lax.all_to_all(
        halves, BOTH, 0, 0, axis_index_groups=chip_groups(), tiled=True
    )
    united, latent_grad = tail_kernel(
        tokens, act, uniting_out, up_cot.reshape(fine_tokens.shape), up_cot_edge,
        above, below, upsample_weight,
    )
    in_grad, out_grad = sum_blocks(parts)
    return (
        united.reshape(fine_tokens.shape),
        latent_grad.reshape(latents.shape),
        in_grad,
        out_grad,
    )


def solution(mesh):
    return jax.shard_map(
        shards,
        mesh=mesh,
        in_specs=(
            P("lat", "lon", None),
            P("lat", "lon", None),
            P(),
            P(),
            P(),
            P("lat", "lon", None),
        ),
        out_specs=(P("lat", "lon", None), P("lat", "lon", None), P("lon", "lat"), P("lon", "lat")),
        check_vma=False,
    )
```

```python
import jax
import jax.numpy as jnp
from jax import lax
from jax.experimental import pallas as pl
from jax.experimental.pallas import tpu as pltpu
from jax.sharding import PartitionSpec as P

BF16 = jnp.bfloat16
F32 = jnp.float32
BOTH = ("lat", "lon")
GRANT = 46


def dot_nn(a, b):
    return lax.dot_general(a, b, (((1,), (0,)), ((), ())), preferred_element_type=F32)


def dot_nt(a, b):
    return lax.dot_general(a, b, (((1,), (1,)), ((), ())), preferred_element_type=F32)


def cost(flops, nbytes):
    return pl.CostEstimate(flops=flops, bytes_accessed=nbytes, transcendentals=0)


def iota(shape, dim):
    return lax.broadcasted_iota(jnp.int32, shape, dim)


def main_body(
    core, lat, before, after, left, right, w_a, w_b, tokens, cot, w_in_hbm, w_out_hbm,
    act_out, up_cot, up_cot_edge, first_row, last_row, keep, send,
    sources, edges, tokens_edge, cot_edge, w_in, w_out, up, act, pre, pre_edge,
    turned, sems,
):
    step = pl.program_id(0)
    rows, cols, width = lat.shape
    hidden, model = w_out.shape
    half_model = model // 2
    block = act_out.shape[0]
    count = act.shape[0]
    fine_cols = 2 * cols
    copies = [
        pltpu.make_async_copy(source, target, sems.at[i])
        for i, (source, target) in enumerate(
            ((w_in_hbm, w_in), (w_out_hbm, w_out))
        )
    ]

    @pl.when(step == 1)
    def _():
        for copy in copies:
            copy.start()

    @pl.when(step == 0)
    def _():
        lefts, rights = left[0:16].astype(F32), right[0:16].astype(F32)
        edges[...] = jnp.zeros_like(edges)
        place = iota((cols, width), 0)
        for r in range(rows + 2):
            row = before[0:cols] if r == 0 else after[0:cols] if r == rows + 1 else lat[r - 1]
            wide = row.astype(F32)
            at = slice(16 + r * cols, 16 + (r + 1) * cols)
            sources[0, at] = row
            sources[1, at] = jnp.where(
                place == 0, lefts[r : r + 1], pltpu.roll(wide, 1, 0)
            ).astype(BF16)
            sources[2, at] = jnp.where(
                place == cols - 1, rights[r : r + 1], pltpu.roll(wide, cols - 1, 0)
            ).astype(BF16)
            sources[3, at] = row
            edges[0, r : r + 1] = wide[cols - 1 : cols]
            edges[1, r : r + 1] = wide[0:1]
        last = 16 + (rows + 2) * cols
        for i, edge in enumerate((rights, edges[0], edges[1], lefts)):
            sources[i, 0:16] = edge.astype(BF16)
            sources[i, last : last + 16] = pltpu.roll(edge, 15, 0).astype(BF16)
        for ref, part in ((tokens_edge, 16), (cot_edge, 48)):
            ref[0:32] = left[part : part + 32]
            ref[32:] = right[part : part + 32]

    @pl.when(step < 4)
    def _():
        parity, half = step // 2, step % 2
        size = (rows + 1) * cols
        planes = []
        for q, taps in enumerate((((1, 0), (3, 1)), ((0, 2), (2, 3)))):
            total_a = total_b = None
            for tap, i in taps:
                term_a = dot_nt(sources[i, 16 + cols : 32 + cols + size], w_a[0, tap])
                term_b = dot_nt(sources[i, 0 : 16 + size], w_b[0, tap])
                total_a = term_a if total_a is None else total_a + term_a
                total_b = term_b if total_b is None else total_b + term_b
            planes.append((total_a[:size] + total_b[16:]).astype(BF16))
            side = (total_a[size:] + total_b[:16]).astype(BF16)
            at = count + fine_cols + (1 - q) * 32 + (1 - parity) * 16
            up[half, pl.ds(pl.multiple_of(at, 16), 16)] = side
        r, k = iota((fine_cols, fine_cols), 0), iota((fine_cols, fine_cols), 1)
        spread = (k == (r % 2) * cols + r // 2).astype(F32).astype(BF16)
        for m in range(rows + 1):
            pair = jnp.concatenate([z[m * cols : (m + 1) * cols] for z in planes], axis=0)
            value = dot_nn(spread, pair).astype(BF16)
            even = 2 * m * fine_cols if m < rows else count
            odd = (2 * m - 1) * fine_cols if m > 0 else count
            at = even + parity * (odd - even)
            up[half, pl.ds(pl.multiple_of(at, 128), fine_cols)] = value

    @pl.when(step == 4)
    def _():
        for copy in copies:
            copy.wait()

    def network(tokens_of, up_of, cot_of, span):
        h = dot_nn(tokens_of(), w_in[:model, span])
        h += dot_nn(up_of(0), w_in[model : model + half_model, span])
        h += dot_nn(up_of(1), w_in[model + half_model :, span])
        g = 0.5 * jnp.tanh(0.5 * h) + 0.5
        y = h * g
        a = dot_nt(cot_of(), w_out[span, :])
        return y.astype(BF16), (a * (g + y * (1.0 - g))).astype(BF16)

    @pl.when(step == 4)
    def _():
        for n in range(0, hidden, 256):
            span = slice(n, n + 256)
            _, pre_edge[:, span] = network(
                lambda: tokens_edge[...], lambda i: up[i, count + fine_cols :], lambda: cot_edge[...], span
            )
        value = dot_nt(pre_edge[...], w_in[model:, :]).astype(BF16)
        up_cot_edge[...] = value
        for i in range(2):
            at = slice(fine_cols + 16 * i, fine_cols + 16 * i + 16)
            last_row[at] = value[32 * i : 32 * i + 16]
            first_row[at] = value[32 * i + 16 : 32 * i + 32]

    @pl.when((step > 4) & (step < 9))
    def _():
        at = pl.ds(pl.multiple_of((step - 5) * block, block), block)
        for n in range(0, hidden, 256):
            span = slice(n, n + 256)
            wide, grad = network(
                lambda: tokens[...], lambda i: up[i, at], lambda: cot[...], span
            )
            act[at, span] = wide
            act_out[:, span] = wide
            pre[at, span] = grad
        turned[0:model, at] = tokens[...].T
        turned[model : model + half_model, at] = up[0, at].T
        turned[model + half_model : 2 * model, at] = up[1, at].T
        turned[2 * model :, at] = cot[...].T
        up_cot[...] = dot_nt(pre[at, :], w_in[model:, :]).astype(BF16)

    @pl.when(step == 5)
    def _():
        first_row[0:fine_cols] = up_cot[0:fine_cols]

    @pl.when(step == 8)
    def _():
        last_row[0:fine_cols] = up_cot[block - fine_cols :]

    for j in range(4):

        @pl.when(step == 9 + j)
        def _():
            span = slice(j * 256, (j + 1) * 256)
            mine = core[0]
            total = dot_nn(turned[: 2 * model], pre[:, span])
            for z in range(4):
                for y_hi in range(2):
                    base = (z * 2 + y_hi) * 128
                    first, second = total[base : base + 64], total[base + 64 : base + 128]
                    own = jnp.where(mine == 0, first, second).astype(BF16)
                    other = jnp.where(mine == 0, second, first).astype(BF16)
                    for y_lo in range(2):
                        lanes = slice(y_lo * 128, (y_lo + 1) * 128)
                        keep[z, j, y_hi * 2 + y_lo, 0:64] = own[:, lanes]
                        send[z, j, y_hi * 2 + y_lo, 0:64] = other[:, lanes]
            total = dot_nn(turned[2 * model :], act[:, span])
            low = iota((32, 128), 1) < 64
            for lat_id in range(8):
                for y_hi in range(2):
                    lanes = slice(y_hi * 128, (y_hi + 1) * 128)
                    a = total[lat_id * 64 : lat_id * 64 + 32, lanes]
                    b = total[lat_id * 64 + 32 : lat_id * 64 + 64, lanes]
                    first = jnp.where(low, a, pltpu.roll(b, 64, 1))
                    second = jnp.where(low, pltpu.roll(a, 64, 1), b)
                    at = y_hi * 2 + lat_id % 2
                    keep[j, lat_id // 2, at, 64:96] = jnp.where(
                        mine == 0, first, second
                    ).astype(BF16)
                    send[j, lat_id // 2, at, 64:96] = jnp.where(
                        mine == 0, second, first
                    ).astype(BF16)


def main_kernel(core, lat, before, after, left, right, weight, tokens, cot, w_in, w_out):
    rows, cols, width = lat.shape
    model = weight.shape[0] // 16
    half = model // 2
    count = tokens.shape[0]
    hidden = w_out.shape[0]
    block = count // 4
    edge = 64
    pack = 2 * cols + 32
    clamp = lambda i, low: jnp.clip(i - low, 0, 3)
    whole = lambda *shape: pl.BlockSpec(shape, lambda i, c: (0,) * len(shape))
    kernel_row = lambda i, top: (top - clamp(i, 0) // 2, 0, clamp(i, 0) % 2, 0)
    tokens_of = lambda w: pl.BlockSpec((block, w), lambda i, c: (clamp(i, 5), 0))
    blocks = (4, 4, 4, 96, 128)
    return pl.pallas_call(
        main_body,
        grid_spec=pltpu.PrefetchScalarGridSpec(
            num_scalar_prefetch=1,
            grid=(13,),
            in_specs=[
                whole(rows, cols, width),
                whole(*before.shape),
                whole(*after.shape),
                whole(*left.shape),
                whole(*right.shape),
                pl.BlockSpec((1, 4, half, width), lambda i, c: kernel_row(i, 1)),
                pl.BlockSpec((1, 4, half, width), lambda i, c: kernel_row(i, 3)),
                tokens_of(model),
                tokens_of(model),
                pl.BlockSpec(memory_space=pl.ANY),
                pl.BlockSpec(memory_space=pl.ANY),
            ],
            out_specs=[
                tokens_of(hidden),
                tokens_of(model),
                whole(edge, model),
                whole(pack, model),
                whole(pack, model),
                whole(*blocks),
                whole(*blocks),
            ],
            scratch_shapes=[
                pltpu.VMEM((4, (rows + 2) * cols + 32, width), BF16),
                pltpu.VMEM((2, 16, width), F32),
                pltpu.VMEM((edge, model), BF16),
                pltpu.VMEM((edge, model), BF16),
                pltpu.VMEM((2 * model, hidden), BF16),
                pltpu.VMEM((hidden, model), BF16),
                pltpu.VMEM((2, count + 2 * cols + edge, half), BF16),
                pltpu.VMEM((count, hidden), BF16),
                pltpu.VMEM((count, hidden), BF16),
                pltpu.VMEM((edge, hidden), BF16),
                pltpu.VMEM((3 * model, count), BF16),
                pltpu.SemaphoreType.DMA((2,)),
            ],
        ),
        out_shape=[
            jax.ShapeDtypeStruct((count, hidden), BF16),
            jax.ShapeDtypeStruct((count, model), BF16),
            jax.ShapeDtypeStruct((edge, model), BF16),
            jax.ShapeDtypeStruct((pack, model), BF16),
            jax.ShapeDtypeStruct((pack, model), BF16),
            jax.ShapeDtypeStruct(blocks, BF16),
            jax.ShapeDtypeStruct(blocks, BF16),
        ],
        compiler_params=pltpu.CompilerParams(vmem_limit_bytes=GRANT << 20),
        cost_estimate=cost(20 << 30, 36 << 20),
        name="main",
    )(
        core, lat, before, after, left, right, *[weight.reshape(4, 4, model, width)] * 2,
        tokens, cot, w_in, w_out,
    )


def tail_body(
    tokens, act, w_out, cot_hbm, edge, before, after, weight, united, out,
    cot, planes, sem,
):
    step = pl.program_id(0)
    fine_rows, fine_cols, model = cot.shape
    cols = fine_cols // 2
    rows = fine_rows // 2
    copy = pltpu.make_async_copy(cot_hbm, cot, sem.at[0])

    @pl.when(step == 0)
    def _():
        copy.start()

    @pl.when(step < 4)
    def _():
        united[...] = (tokens[...].astype(F32) + dot_nn(act[...], w_out[...])).astype(BF16)

    @pl.when(step == 4)
    def _():
        copy.wait()
        r, c = iota((fine_cols, fine_cols), 0), iota((fine_cols, fine_cols), 1)
        pick = (c == 2 * (r % cols) + r // cols).astype(F32).astype(BF16)
        sides, above, below = [ref.astype(F32) for ref in (
            edge[...], before[fine_cols:], after[fine_cols:]
        )]
        place = iota((cols, model), 0)
        for e in range(fine_rows + 2):
            if e == 0:
                row, left, right = before[0:fine_cols], above[8:9], above[24:25]
            elif e == fine_rows + 1:
                row, left, right = after[0:fine_cols], below[0:1], below[16:17]
            else:
                at = e // 2 + 16 * (e % 2)
                row, left, right = cot[e - 1], sides[at : at + 1], sides[at + 32 : at + 33]
            found = dot_nn(pick, row)
            even, odd = found[:cols], found[cols:]
            taps = (
                jnp.where(place == 0, left, pltpu.roll(odd, 1, 0)),
                even,
                odd,
                jnp.where(place == cols - 1, right, pltpu.roll(even, cols - 1, 0)),
            )
            for tap in range(4):
                planes[e % 2, e // 2, :, tap * model : (tap + 1) * model] = taps[tap].astype(BF16)

    @pl.when(step >= 4)
    def _():
        k = step - 4
        source = planes[k % 2, pl.ds(k // 2, rows)].reshape(rows * cols, 4 * model)
        term = dot_nn(source, weight[0])

        @pl.when(k == 0)
        def _():
            out[...] = term

        @pl.when(k != 0)
        def _():
            out[...] += term


def tail_kernel(tokens, act, w_out, cot, edge, before, after, weight):
    fine_rows, fine_cols, model = cot.shape
    width = weight.shape[1]
    count, hidden = act.shape
    block = count // 4
    whole = lambda a: pl.BlockSpec(a.shape, lambda i: (0,) * a.ndim)
    size = fine_rows * fine_cols // 4
    tokens_of = lambda w: pl.BlockSpec((block, w), lambda i: (jnp.minimum(i, 3), 0))
    return pl.pallas_call(
        tail_body,
        grid=(8,),
        in_specs=[
            tokens_of(model),
            tokens_of(hidden),
            whole(w_out),
            pl.BlockSpec(memory_space=pl.ANY),
            whole(edge),
            whole(before),
            whole(after),
            pl.BlockSpec((1, 4 * model, width), lambda i: (jnp.maximum(i - 4, 0), 0, 0)),
        ],
        out_specs=[tokens_of(model), pl.BlockSpec((size, width), lambda i: (0, 0))],
        out_shape=[
            jax.ShapeDtypeStruct((count, model), BF16),
            jax.ShapeDtypeStruct((size, width), F32),
        ],
        scratch_shapes=[
            pltpu.VMEM((fine_rows, fine_cols, model), BF16),
            pltpu.VMEM((2, fine_rows // 2 + 1, fine_cols // 2, 4 * model), BF16),
            pltpu.SemaphoreType.DMA((1,)),
        ],
        compiler_params=pltpu.CompilerParams(vmem_limit_bytes=58 << 20),
        cost_estimate=cost(7 << 30, 22 << 20),
        name="tail",
    )(tokens, act, w_out, cot, edge, before, after, weight.reshape(4, 4 * model, width))


def sum_body(parts, in_grad, out_grad):
    total = parts[0].astype(F32)
    for i in range(1, parts.shape[0]):
        total = total + parts[i].astype(F32)
    in_grad[...] = total[:64]
    packed = total[64:]
    out_grad[...] = jnp.concatenate(
        [packed, pltpu.roll(packed, 64, 1)], axis=0
    ).T[:64, :]


def sum_blocks(parts):
    return pl.pallas_call(
        sum_body,
        out_shape=[
            jax.ShapeDtypeStruct((64, 128), F32),
            jax.ShapeDtypeStruct((64, 64), F32),
        ],
        compiler_params=pltpu.CompilerParams(vmem_limit_bytes=8 << 20),
        cost_estimate=cost(1 << 20, 2 << 20),
        name="sum_blocks",
    )(parts)


def swap(last, first, axis, wrap):
    devices = lax.axis_size(axis)
    up = [(i, (i + 1) % devices) for i in range(devices if wrap else devices - 1)]
    down = [(j, i) for i, j in up]
    return lax.ppermute(last, axis, up), lax.ppermute(first, axis, down)


def halos(latents, tokens, cot):
    before, after = swap(latents[-1], latents[0], "lat", False)

    def column(c):
        place = c % latents.shape[1]
        ends = [a[place : place + 1] for a in (before, after)]
        parts = [ends[0], latents[:, c], ends[1], jnp.zeros((6, latents.shape[2]), BF16)]
        for fine in (tokens, cot):
            parts.append(jnp.pad(fine[1::2, c], ((1, 7), (0, 0))))
            parts.append(jnp.pad(fine[0::2, c], ((0, 8), (0, 0))))
        return jnp.concatenate(parts, axis=0)

    left, right = swap(column(-1), column(0), "lon", True)
    return before, after, left, right


def chip_groups():
    return [
        [
            (x * 2 + y_lo) * 16 + z * 4 + y_hi * 2 + core
            for z in range(4)
            for x in range(4)
            for y_hi in range(2)
            for y_lo in range(2)
        ]
        for core in range(2)
    ]


def other_core(array):
    return lax.ppermute(array, "lon", [(i, i ^ 1) for i in range(16)])


def shards(fine_tokens, latents, upsample_weight, uniting_in, uniting_out, cotangent):
    count = fine_tokens.shape[0] * fine_tokens.shape[1]
    model = fine_tokens.shape[2]
    core = (lax.axis_index("lon") % 2).astype(jnp.int32).reshape(1)
    tokens = fine_tokens.reshape(count, model)
    cot = cotangent.reshape(count, model)

    before, after, left, right = halos(latents, fine_tokens, cotangent)
    act, up_cot, up_cot_edge, first_row, last_row, keep, send = main_kernel(
        core, latents, before, after, left, right, upsample_weight,
        tokens, cot, uniting_in, uniting_out,
    )
    other = other_core(send)
    above, below = swap(last_row, first_row, "lat", False)
    halves = (keep.astype(F32) + other.astype(F32)).astype(BF16).reshape(64, 96, 128)
    parts = lax.all_to_all(
        halves, BOTH, 0, 0, axis_index_groups=chip_groups(), tiled=True
    )
    united, latent_grad = tail_kernel(
        tokens, act, uniting_out, up_cot.reshape(fine_tokens.shape), up_cot_edge,
        above, below, upsample_weight,
    )
    in_grad, out_grad = sum_blocks(parts)
    return (
        united.reshape(fine_tokens.shape),
        latent_grad.reshape(latents.shape),
        in_grad,
        out_grad,
    )


def solution(mesh):
    return jax.shard_map(
        shards,
        mesh=mesh,
        in_specs=(
            P("lat", "lon", None),
            P("lat", "lon", None),
            P(),
            P(),
            P(),
            P("lat", "lon", None),
        ),
        out_specs=(P("lat", "lon", None), P("lat", "lon", None), P("lon", "lat"), P("lon", "lat")),
        check_vma=False,
    )
```

```python
import jax
import jax.numpy as jnp
from jax import lax
from jax.experimental import pallas as pl
from jax.experimental.pallas import tpu as pltpu
from jax.sharding import PartitionSpec as P

BF16 = jnp.bfloat16
F32 = jnp.float32
BOTH = ("lat", "lon")
GRANT = 46


def dot_nn(a, b):
    return lax.dot_general(a, b, (((1,), (0,)), ((), ())), preferred_element_type=F32)


def dot_nt(a, b):
    return lax.dot_general(a, b, (((1,), (1,)), ((), ())), preferred_element_type=F32)


def cost(flops, nbytes):
    return pl.CostEstimate(flops=flops, bytes_accessed=nbytes, transcendentals=0)


def iota(shape, dim):
    return lax.broadcasted_iota(jnp.int32, shape, dim)


def main_body(
    core, lat, before, after, left, right, w_a, w_b, tokens, cot, w_in_hbm, w_out_hbm,
    act_out, up_cot, up_cot_edge, first_row, last_row, keep, send,
    sources, edges, tokens_edge, cot_edge, w_in, w_out, up, act, pre, pre_edge,
    turned, sems,
):
    step = pl.program_id(0)
    rows, cols, width = lat.shape
    hidden, model = w_out.shape
    half_model = model // 2
    block = act_out.shape[0]
    count = act.shape[0]
    fine_cols = 2 * cols
    copies = [
        pltpu.make_async_copy(source, target, sems.at[i])
        for i, (source, target) in enumerate(
            ((w_in_hbm, w_in), (w_out_hbm, w_out))
        )
    ]

    @pl.when(step == 1)
    def _():
        for copy in copies:
            copy.start()

    @pl.when(step == 0)
    def _():
        lefts, rights = left[0:16].astype(F32), right[0:16].astype(F32)
        edges[...] = jnp.zeros_like(edges)
        place = iota((cols, width), 0)
        for r in range(rows + 2):
            row = before[0:cols] if r == 0 else after[0:cols] if r == rows + 1 else lat[r - 1]
            wide = row.astype(F32)
            at = slice(16 + r * cols, 16 + (r + 1) * cols)
            sources[0, at] = row
            sources[1, at] = jnp.where(
                place == 0, lefts[r : r + 1], pltpu.roll(wide, 1, 0)
            ).astype(BF16)
            sources[2, at] = jnp.where(
                place == cols - 1, rights[r : r + 1], pltpu.roll(wide, cols - 1, 0)
            ).astype(BF16)
            sources[3, at] = row
            edges[0, r : r + 1] = wide[cols - 1 : cols]
            edges[1, r : r + 1] = wide[0:1]
        last = 16 + (rows + 2) * cols
        for i, edge in enumerate((rights, edges[0], edges[1], lefts)):
            sources[i, 0:16] = edge.astype(BF16)
            sources[i, last : last + 16] = pltpu.roll(edge, 15, 0).astype(BF16)
        for ref, part in ((tokens_edge, 16), (cot_edge, 48)):
            ref[0:32] = left[part : part + 32]
            ref[32:] = right[part : part + 32]

    @pl.when(step < 4)
    def _():
        parity, half = step // 2, step % 2
        size = (rows + 1) * cols
        planes = []
        for q, taps in enumerate((((1, 0), (3, 1)), ((0, 2), (2, 3)))):
            total_a = total_b = None
            for tap, i in taps:
                term_a = dot_nt(sources[i, 16 + cols : 32 + cols + size], w_a[0, tap])
                term_b = dot_nt(sources[i, 0 : 16 + size], w_b[0, tap])
                total_a = term_a if total_a is None else total_a + term_a
                total_b = term_b if total_b is None else total_b + term_b
            planes.append((total_a[:size] + total_b[16:]).astype(BF16))
            side = (total_a[size:] + total_b[:16]).astype(BF16)
            at = count + fine_cols + (1 - q) * 32 + (1 - parity) * 16
            up[half, pl.ds(pl.multiple_of(at, 16), 16)] = side
        r, k = iota((fine_cols, fine_cols), 0), iota((fine_cols, fine_cols), 1)
        spread = (k == (r % 2) * cols + r // 2).astype(F32).astype(BF16)
        for m in range(rows + 1):
            pair = jnp.concatenate([z[m * cols : (m + 1) * cols] for z in planes], axis=0)
            value = dot_nn(spread, pair).astype(BF16)
            even = 2 * m * fine_cols if m < rows else count
            odd = (2 * m - 1) * fine_cols if m > 0 else count
            at = even + parity * (odd - even)
            up[half, pl.ds(pl.multiple_of(at, 128), fine_cols)] = value

    @pl.when(step == 4)
    def _():
        for copy in copies:
            copy.wait()

    def network(tokens_of, up_of, cot_of, span):
        h = dot_nn(tokens_of(), w_in[:model, span])
        h += dot_nn(up_of(0), w_in[model : model + half_model, span])
        h += dot_nn(up_of(1), w_in[model + half_model :, span])
        g = 0.5 * jnp.tanh(0.5 * h) + 0.5
        y = h * g
        a = dot_nt(cot_of(), w_out[span, :])
        return y.astype(BF16), (a * (g + y * (1.0 - g))).astype(BF16)

    @pl.when(step == 4)
    def _():
        for n in range(0, hidden, 256):
            span = slice(n, n + 256)
            _, pre_edge[:, span] = network(
                lambda: tokens_edge[...], lambda i: up[i, count + fine_cols :], lambda: cot_edge[...], span
            )
        value = dot_nt(pre_edge[...], w_in[model:, :]).astype(BF16)
        up_cot_edge[...] = value
        for i in range(2):
            at = slice(fine_cols + 16 * i, fine_cols + 16 * i + 16)
            last_row[at] = value[32 * i : 32 * i + 16]
            first_row[at] = value[32 * i + 16 : 32 * i + 32]

    @pl.when((step > 4) & (step < 9))
    def _():
        at = pl.ds(pl.multiple_of((step - 5) * block, block), block)
        for n in range(0, hidden, 256):
            span = slice(n, n + 256)
            wide, grad = network(
                lambda: tokens[...], lambda i: up[i, at], lambda: cot[...], span
            )
            act[at, span] = wide
            act_out[:, span] = wide
            pre[at, span] = grad
        turned[0:model, at] = tokens[...].T
        turned[model : model + half_model, at] = up[0, at].T
        turned[model + half_model : 2 * model, at] = up[1, at].T
        turned[2 * model :, at] = cot[...].T
        up_cot[...] = dot_nt(pre[at, :], w_in[model:, :]).astype(BF16)

    @pl.when(step == 5)
    def _():
        first_row[0:fine_cols] = up_cot[0:fine_cols]

    @pl.when(step == 8)
    def _():
        last_row[0:fine_cols] = up_cot[block - fine_cols :]

    for j in range(4):

        @pl.when(step == 9 + j)
        def _():
            span = slice(j * 256, (j + 1) * 256)
            mine = core[0]
            total = dot_nn(turned[: 2 * model], pre[:, span])
            for z in range(4):
                for y_hi in range(2):
                    base = (z * 2 + y_hi) * 128
                    first, second = total[base : base + 64], total[base + 64 : base + 128]
                    own = jnp.where(mine == 0, first, second).astype(BF16)
                    other = jnp.where(mine == 0, second, first).astype(BF16)
                    for y_lo in range(2):
                        lanes = slice(y_lo * 128, (y_lo + 1) * 128)
                        keep[z, j, y_hi * 2 + y_lo, 0:64] = own[:, lanes]
                        send[z, j, y_hi * 2 + y_lo, 0:64] = other[:, lanes]
            total = dot_nn(turned[2 * model :], act[:, span])
            low = iota((32, 128), 1) < 64
            for lat_id in range(8):
                for y_hi in range(2):
                    lanes = slice(y_hi * 128, (y_hi + 1) * 128)
                    a = total[lat_id * 64 : lat_id * 64 + 32, lanes]
                    b = total[lat_id * 64 + 32 : lat_id * 64 + 64, lanes]
                    first = jnp.where(low, a, pltpu.roll(b, 64, 1))
                    second = jnp.where(low, pltpu.roll(a, 64, 1), b)
                    at = y_hi * 2 + lat_id % 2
                    keep[j, lat_id // 2, at, 64:96] = jnp.where(
                        mine == 0, first, second
                    ).astype(BF16)
                    send[j, lat_id // 2, at, 64:96] = jnp.where(
                        mine == 0, second, first
                    ).astype(BF16)


def main_kernel(core, lat, before, after, left, right, weight, tokens, cot, w_in, w_out):
    rows, cols, width = lat.shape
    model = weight.shape[0] // 16
    half = model // 2
    count = tokens.shape[0]
    hidden = w_out.shape[0]
    block = count // 4
    edge = 64
    pack = 2 * cols + 32
    clamp = lambda i, low: jnp.clip(i - low, 0, 3)
    whole = lambda *shape: pl.BlockSpec(shape, lambda i, c: (0,) * len(shape))
    kernel_row = lambda i, top: (top - clamp(i, 0) // 2, 0, clamp(i, 0) % 2, 0)
    tokens_of = lambda w: pl.BlockSpec((block, w), lambda i, c: (clamp(i, 5), 0))
    blocks = (4, 4, 4, 96, 128)
    return pl.pallas_call(
        main_body,
        grid_spec=pltpu.PrefetchScalarGridSpec(
            num_scalar_prefetch=1,
            grid=(13,),
            in_specs=[
                whole(rows, cols, width),
                whole(*before.shape),
                whole(*after.shape),
                whole(*left.shape),
                whole(*right.shape),
                pl.BlockSpec((1, 4, half, width), lambda i, c: kernel_row(i, 1)),
                pl.BlockSpec((1, 4, half, width), lambda i, c: kernel_row(i, 3)),
                tokens_of(model),
                tokens_of(model),
                pl.BlockSpec(memory_space=pltpu.HBM),
                pl.BlockSpec(memory_space=pltpu.HBM),
            ],
            out_specs=[
                tokens_of(hidden),
                tokens_of(model),
                whole(edge, model),
                whole(pack, model),
                whole(pack, model),
                whole(*blocks),
                whole(*blocks),
            ],
            scratch_shapes=[
                pltpu.VMEM((4, (rows + 2) * cols + 32, width), BF16),
                pltpu.VMEM((2, 16, width), F32),
                pltpu.VMEM((edge, model), BF16),
                pltpu.VMEM((edge, model), BF16),
                pltpu.VMEM((2 * model, hidden), BF16),
                pltpu.VMEM((hidden, model), BF16),
                pltpu.VMEM((2, count + 2 * cols + edge, half), BF16),
                pltpu.VMEM((count, hidden), BF16),
                pltpu.VMEM((count, hidden), BF16),
                pltpu.VMEM((edge, hidden), BF16),
                pltpu.VMEM((3 * model, count), BF16),
                pltpu.SemaphoreType.DMA((2,)),
            ],
        ),
        out_shape=[
            jax.ShapeDtypeStruct((count, hidden), BF16),
            jax.ShapeDtypeStruct((count, model), BF16),
            jax.ShapeDtypeStruct((edge, model), BF16),
            jax.ShapeDtypeStruct((pack, model), BF16),
            jax.ShapeDtypeStruct((pack, model), BF16),
            jax.ShapeDtypeStruct(blocks, BF16),
            jax.ShapeDtypeStruct(blocks, BF16),
        ],
        compiler_params=pltpu.CompilerParams(vmem_limit_bytes=GRANT << 20),
        cost_estimate=cost(20 << 30, 36 << 20),
        name="main",
    )(
        core, lat, before, after, left, right, *[weight.reshape(4, 4, model, width)] * 2,
        tokens, cot, w_in, w_out,
    )


def tail_body(
    tokens, act, w_out, cot_hbm, edge, before, after, weight, united, out,
    cot, planes, sem,
):
    step = pl.program_id(0)
    fine_rows, fine_cols, model = cot.shape
    cols = fine_cols // 2
    rows = fine_rows // 2
    copy = pltpu.make_async_copy(cot_hbm, cot, sem.at[0])

    @pl.when(step == 0)
    def _():
        copy.start()

    @pl.when(step < 4)
    def _():
        united[...] = (tokens[...].astype(F32) + dot_nn(act[...], w_out[...])).astype(BF16)

    @pl.when(step == 4)
    def _():
        copy.wait()
        r, c = iota((fine_cols, fine_cols), 0), iota((fine_cols, fine_cols), 1)
        pick = (c == 2 * (r % cols) + r // cols).astype(F32).astype(BF16)
        sides, above, below = [ref.astype(F32) for ref in (
            edge[...], before[fine_cols:], after[fine_cols:]
        )]
        place = iota((cols, model), 0)
        for e in range(fine_rows + 2):
            if e == 0:
                row, left, right = before[0:fine_cols], above[8:9], above[24:25]
            elif e == fine_rows + 1:
                row, left, right = after[0:fine_cols], below[0:1], below[16:17]
            else:
                at = e // 2 + 16 * (e % 2)
                row, left, right = cot[e - 1], sides[at : at + 1], sides[at + 32 : at + 33]
            found = dot_nn(pick, row)
            even, odd = found[:cols], found[cols:]
            taps = (
                jnp.where(place == 0, left, pltpu.roll(odd, 1, 0)),
                even,
                odd,
                jnp.where(place == cols - 1, right, pltpu.roll(even, cols - 1, 0)),
            )
            for tap in range(4):
                planes[e % 2, e // 2, :, tap * model : (tap + 1) * model] = taps[tap].astype(BF16)

    @pl.when(step >= 4)
    def _():
        k = step - 4
        source = planes[k % 2, pl.ds(k // 2, rows)].reshape(rows * cols, 4 * model)
        term = dot_nn(source, weight[0])

        @pl.when(k == 0)
        def _():
            out[...] = term

        @pl.when(k != 0)
        def _():
            out[...] += term


def tail_kernel(tokens, act, w_out, cot, edge, before, after, weight):
    fine_rows, fine_cols, model = cot.shape
    width = weight.shape[1]
    count, hidden = act.shape
    block = count // 4
    whole = lambda a: pl.BlockSpec(a.shape, lambda i: (0,) * a.ndim)
    size = fine_rows * fine_cols // 4
    tokens_of = lambda w: pl.BlockSpec((block, w), lambda i: (jnp.minimum(i, 3), 0))
    return pl.pallas_call(
        tail_body,
        grid=(8,),
        in_specs=[
            tokens_of(model),
            tokens_of(hidden),
            whole(w_out),
            pl.BlockSpec(memory_space=pl.ANY),
            whole(edge),
            whole(before),
            whole(after),
            pl.BlockSpec((1, 4 * model, width), lambda i: (jnp.maximum(i - 4, 0), 0, 0)),
        ],
        out_specs=[tokens_of(model), pl.BlockSpec((size, width), lambda i: (0, 0))],
        out_shape=[
            jax.ShapeDtypeStruct((count, model), BF16),
            jax.ShapeDtypeStruct((size, width), F32),
        ],
        scratch_shapes=[
            pltpu.VMEM((fine_rows, fine_cols, model), BF16),
            pltpu.VMEM((2, fine_rows // 2 + 1, fine_cols // 2, 4 * model), BF16),
            pltpu.SemaphoreType.DMA((1,)),
        ],
        compiler_params=pltpu.CompilerParams(vmem_limit_bytes=58 << 20),
        cost_estimate=cost(7 << 30, 22 << 20),
        name="tail",
    )(tokens, act, w_out, cot, edge, before, after, weight.reshape(4, 4 * model, width))


def sum_body(parts, in_grad, out_grad):
    total = parts[0].astype(F32)
    for i in range(1, parts.shape[0]):
        total = total + parts[i].astype(F32)
    in_grad[...] = total[:64]
    packed = total[64:]
    out_grad[...] = jnp.concatenate(
        [packed, pltpu.roll(packed, 64, 1)], axis=0
    ).T[:64, :]


def sum_blocks(parts):
    return pl.pallas_call(
        sum_body,
        out_shape=[
            jax.ShapeDtypeStruct((64, 128), F32),
            jax.ShapeDtypeStruct((64, 64), F32),
        ],
        compiler_params=pltpu.CompilerParams(vmem_limit_bytes=8 << 20),
        cost_estimate=cost(1 << 20, 2 << 20),
        name="sum_blocks",
    )(parts)


def swap(last, first, axis, wrap):
    devices = lax.axis_size(axis)
    up = [(i, (i + 1) % devices) for i in range(devices if wrap else devices - 1)]
    down = [(j, i) for i, j in up]
    one = lax.ppermute(last, axis, up)
    other = lax.ppermute(first, axis, down)
    return one, other


def halos(latents, tokens, cot):
    before, after = swap(latents[-1], latents[0], "lat", False)

    def column(c):
        place = c % latents.shape[1]
        ends = [a[place : place + 1] for a in (before, after)]
        parts = [ends[0], latents[:, c], ends[1], jnp.zeros((6, latents.shape[2]), BF16)]
        for fine in (tokens, cot):
            parts.append(jnp.pad(fine[1::2, c], ((1, 7), (0, 0))))
            parts.append(jnp.pad(fine[0::2, c], ((0, 8), (0, 0))))
        return jnp.concatenate(parts, axis=0)

    left, right = swap(column(-1), column(0), "lon", True)
    return before, after, left, right


def chip_groups():
    return [
        [
            (x * 2 + y_lo) * 16 + z * 4 + y_hi * 2 + core
            for z in range(4)
            for x in range(4)
            for y_hi in range(2)
            for y_lo in range(2)
        ]
        for core in range(2)
    ]


def other_core(array):
    return lax.ppermute(array, "lon", [(i, i ^ 1) for i in range(16)])


def shards(fine_tokens, latents, upsample_weight, uniting_in, uniting_out, cotangent):
    count = fine_tokens.shape[0] * fine_tokens.shape[1]
    model = fine_tokens.shape[2]
    core = (lax.axis_index("lon") % 2).astype(jnp.int32).reshape(1)
    tokens = fine_tokens.reshape(count, model)
    cot = cotangent.reshape(count, model)

    before, after, left, right = halos(latents, fine_tokens, cotangent)
    act, up_cot, up_cot_edge, first_row, last_row, keep, send = main_kernel(
        core, latents, before, after, left, right, upsample_weight,
        tokens, cot, uniting_in, uniting_out,
    )
    other = other_core(send)
    above, below = swap(last_row, first_row, "lat", False)
    halves = (keep.astype(F32) + other.astype(F32)).astype(BF16).reshape(64, 96, 128)
    parts = lax.all_to_all(
        halves, BOTH, 0, 0, axis_index_groups=chip_groups(), tiled=True
    )
    united, latent_grad = tail_kernel(
        tokens, act, uniting_out, up_cot.reshape(fine_tokens.shape), up_cot_edge,
        above, below, upsample_weight,
    )
    in_grad, out_grad = sum_blocks(parts)
    return (
        united.reshape(fine_tokens.shape),
        latent_grad.reshape(latents.shape),
        in_grad,
        out_grad,
    )


def solution(mesh):
    return jax.shard_map(
        shards,
        mesh=mesh,
        in_specs=(
            P("lat", "lon", None),
            P("lat", "lon", None),
            P(),
            P(),
            P(),
            P("lat", "lon", None),
        ),
        out_specs=(P("lat", "lon", None), P("lat", "lon", None), P("lon", "lat"), P("lon", "lat")),
        check_vma=False,
    )
```

```python
import jax
import jax.numpy as jnp
from jax import lax
from jax.experimental import pallas as pl
from jax.experimental.pallas import tpu as pltpu
from jax.sharding import PartitionSpec as P

BF16 = jnp.bfloat16
F32 = jnp.float32
BOTH = ("lat", "lon")
GRANT = 46


def dot_nn(a, b):
    return lax.dot_general(a, b, (((1,), (0,)), ((), ())), preferred_element_type=F32)


def dot_nt(a, b):
    return lax.dot_general(a, b, (((1,), (1,)), ((), ())), preferred_element_type=F32)


def cost(flops, nbytes):
    return pl.CostEstimate(flops=flops, bytes_accessed=nbytes, transcendentals=0)


def iota(shape, dim):
    return lax.broadcasted_iota(jnp.int32, shape, dim)


def main_body(
    core, lat, before, after, left, right, w_a, w_b, tokens, cot, a_own, w_in_hbm, w_out_hbm,
    act_out, up_cot, up_cot_edge, first_row, last_row, keep, send,
    sources, edges, tokens_edge, cot_edge, w_in, w_out, up, act, pre, pre_edge,
    turned, sems,
):
    step = pl.program_id(0)
    rows, cols, width = lat.shape
    hidden, model = w_out.shape
    half_model = model // 2
    block = up_cot.shape[0]
    count = act.shape[0]
    fine_cols = 2 * cols
    copies = [
        pltpu.make_async_copy(source, target, sems.at[i])
        for i, (source, target) in enumerate(
            ((w_in_hbm, w_in), (w_out_hbm, w_out))
        )
    ]

    act_copy = pltpu.make_async_copy(act, act_out, sems.at[2])

    @pl.when(step == 1)
    def _():
        for copy in copies:
            copy.start()

    @pl.when(step == 9)
    def _():
        act_copy.start()

    @pl.when(step == 0)
    def _():
        lefts, rights = left[0:16].astype(F32), right[0:16].astype(F32)
        edges[...] = jnp.zeros_like(edges)
        place = iota((cols, width), 0)
        for r in range(rows + 2):
            row = before[0:cols] if r == 0 else after[0:cols] if r == rows + 1 else lat[r - 1]
            wide = row.astype(F32)
            at = slice(16 + r * cols, 16 + (r + 1) * cols)
            sources[0, at] = row
            sources[1, at] = jnp.where(
                place == 0, lefts[r : r + 1], pltpu.roll(wide, 1, 0)
            ).astype(BF16)
            sources[2, at] = jnp.where(
                place == cols - 1, rights[r : r + 1], pltpu.roll(wide, cols - 1, 0)
            ).astype(BF16)
            sources[3, at] = row
            edges[0, r : r + 1] = wide[cols - 1 : cols]
            edges[1, r : r + 1] = wide[0:1]
        last = 16 + (rows + 2) * cols
        for i, edge in enumerate((rights, edges[0], edges[1], lefts)):
            sources[i, 0:16] = edge.astype(BF16)
            sources[i, last : last + 16] = pltpu.roll(edge, 15, 0).astype(BF16)
        for ref, part in ((tokens_edge, 16), (cot_edge, 48)):
            ref[0:32] = left[part : part + 32]
            ref[32:] = right[part : part + 32]

    @pl.when(step < 4)
    def _():
        parity, half = step // 2, step % 2
        size = (rows + 1) * cols
        planes = []
        for q, taps in enumerate((((1, 0), (3, 1)), ((0, 2), (2, 3)))):
            total_a = total_b = None
            for tap, i in taps:
                term_a = dot_nt(sources[i, 16 + cols : 32 + cols + size], w_a[0, tap])
                term_b = dot_nt(sources[i, 0 : 16 + size], w_b[0, tap])
                total_a = term_a if total_a is None else total_a + term_a
                total_b = term_b if total_b is None else total_b + term_b
            planes.append((total_a[:size] + total_b[16:]).astype(BF16))
            side = (total_a[size:] + total_b[:16]).astype(BF16)
            at = count + fine_cols + (1 - q) * 32 + (1 - parity) * 16
            up[half, pl.ds(pl.multiple_of(at, 16), 16)] = side
        r, k = iota((fine_cols, fine_cols), 0), iota((fine_cols, fine_cols), 1)
        spread = (k == (r % 2) * cols + r // 2).astype(F32).astype(BF16)
        for m in range(rows + 1):
            pair = jnp.concatenate([z[m * cols : (m + 1) * cols] for z in planes], axis=0)
            value = dot_nn(spread, pair).astype(BF16)
            even = 2 * m * fine_cols if m < rows else count
            odd = (2 * m - 1) * fine_cols if m > 0 else count
            at = even + parity * (odd - even)
            up[half, pl.ds(pl.multiple_of(at, 128), fine_cols)] = value

    @pl.when(step == 4)
    def _():
        for copy in copies:
            copy.wait()

    def network(tokens_of, up_of, a_of, span):
        h = dot_nn(tokens_of(), w_in[:model, span])
        h += dot_nn(up_of(0), w_in[model : model + half_model, span])
        h += dot_nn(up_of(1), w_in[model + half_model :, span])
        g = 0.5 * jnp.tanh(0.5 * h) + 0.5
        y = h * g
        a = a_of()
        return y.astype(BF16), (a * (g + y * (1.0 - g))).astype(BF16)

    @pl.when(step == 4)
    def _():
        for n in range(0, hidden, 256):
            span = slice(n, n + 256)
            _, pre_edge[:, span] = network(
                lambda: tokens_edge[...],
                lambda i: up[i, count + fine_cols :],
                lambda: dot_nt(cot_edge[...], w_out[span, :]),
                span,
            )
        value = dot_nt(pre_edge[...], w_in[model:, :]).astype(BF16)
        up_cot_edge[...] = value
        for i in range(2):
            at = slice(fine_cols + 16 * i, fine_cols + 16 * i + 16)
            last_row[at] = value[32 * i : 32 * i + 16]
            first_row[at] = value[32 * i + 16 : 32 * i + 32]

    @pl.when((step > 4) & (step < 9))
    def _():
        at = pl.ds(pl.multiple_of((step - 5) * block, block), block)
        for n in range(0, hidden, 256):
            span = slice(n, n + 256)
            wide, grad = network(
                lambda: tokens[...],
                lambda i: up[i, at],
                lambda: a_own[:, span].astype(F32),
                span,
            )
            act[at, span] = wide
            pre[at, span] = grad
        turned[0:model, at] = tokens[...].T
        turned[model : model + half_model, at] = up[0, at].T
        turned[model + half_model : 2 * model, at] = up[1, at].T
        turned[2 * model :, at] = cot[...].T
        up_cot[...] = dot_nt(pre[at, :], w_in[model:, :]).astype(BF16)

    @pl.when(step == 5)
    def _():
        first_row[0:fine_cols] = up_cot[0:fine_cols]

    @pl.when(step == 8)
    def _():
        last_row[0:fine_cols] = up_cot[block - fine_cols :]

    for j in range(4):

        @pl.when(step == 9 + j)
        def _():
            span = slice(j * 256, (j + 1) * 256)
            mine = core[0]
            total = dot_nn(turned[: 2 * model], pre[:, span])
            for z in range(4):
                for y_hi in range(2):
                    base = (z * 2 + y_hi) * 128
                    first, second = total[base : base + 64], total[base + 64 : base + 128]
                    own = jnp.where(mine == 0, first, second).astype(BF16)
                    other = jnp.where(mine == 0, second, first).astype(BF16)
                    for y_lo in range(2):
                        lanes = slice(y_lo * 128, (y_lo + 1) * 128)
                        keep[z, j, y_hi * 2 + y_lo, 0:64] = own[:, lanes]
                        send[z, j, y_hi * 2 + y_lo, 0:64] = other[:, lanes]
            total = dot_nn(turned[2 * model :], act[:, span])
            low = iota((32, 128), 1) < 64
            for lat_id in range(8):
                for y_hi in range(2):
                    lanes = slice(y_hi * 128, (y_hi + 1) * 128)
                    a = total[lat_id * 64 : lat_id * 64 + 32, lanes]
                    b = total[lat_id * 64 + 32 : lat_id * 64 + 64, lanes]
                    first = jnp.where(low, a, pltpu.roll(b, 64, 1))
                    second = jnp.where(low, pltpu.roll(a, 64, 1), b)
                    at = y_hi * 2 + lat_id % 2
                    keep[j, lat_id // 2, at, 64:96] = jnp.where(
                        mine == 0, first, second
                    ).astype(BF16)
                    send[j, lat_id // 2, at, 64:96] = jnp.where(
                        mine == 0, second, first
                    ).astype(BF16)

    @pl.when(step == 12)
    def _():
        act_copy.wait()


def main_kernel(core, lat, before, after, left, right, weight, tokens, cot, a_own, w_in, w_out):
    rows, cols, width = lat.shape
    model = weight.shape[0] // 16
    half = model // 2
    count = tokens.shape[0]
    hidden = w_out.shape[0]
    block = count // 4
    edge = 64
    pack = 2 * cols + 32
    clamp = lambda i, low: jnp.clip(i - low, 0, 3)
    whole = lambda *shape: pl.BlockSpec(shape, lambda i, c: (0,) * len(shape))
    kernel_row = lambda i, top: (top - clamp(i, 0) // 2, 0, clamp(i, 0) % 2, 0)
    tokens_of = lambda w: pl.BlockSpec((block, w), lambda i, c: (clamp(i, 5), 0))
    blocks = (4, 4, 4, 96, 128)
    return pl.pallas_call(
        main_body,
        grid_spec=pltpu.PrefetchScalarGridSpec(
            num_scalar_prefetch=1,
            grid=(13,),
            in_specs=[
                whole(rows, cols, width),
                whole(*before.shape),
                whole(*after.shape),
                whole(*left.shape),
                whole(*right.shape),
                pl.BlockSpec((1, 4, half, width), lambda i, c: kernel_row(i, 1)),
                pl.BlockSpec((1, 4, half, width), lambda i, c: kernel_row(i, 3)),
                tokens_of(model),
                tokens_of(model),
                tokens_of(hidden),
                pl.BlockSpec(memory_space=pltpu.HBM),
                pl.BlockSpec(memory_space=pltpu.HBM),
            ],
            out_specs=[
                pl.BlockSpec(memory_space=pl.ANY),
                tokens_of(model),
                whole(edge, model),
                whole(pack, model),
                whole(pack, model),
                whole(*blocks),
                whole(*blocks),
            ],
            scratch_shapes=[
                pltpu.VMEM((4, (rows + 2) * cols + 32, width), BF16),
                pltpu.VMEM((2, 16, width), F32),
                pltpu.VMEM((edge, model), BF16),
                pltpu.VMEM((edge, model), BF16),
                pltpu.VMEM((2 * model, hidden), BF16),
                pltpu.VMEM((hidden, model), BF16),
                pltpu.VMEM((2, count + 2 * cols + edge, half), BF16),
                pltpu.VMEM((count, hidden), BF16),
                pltpu.VMEM((count, hidden), BF16),
                pltpu.VMEM((edge, hidden), BF16),
                pltpu.VMEM((3 * model, count), BF16),
                pltpu.SemaphoreType.DMA((3,)),
            ],
        ),
        out_shape=[
            jax.ShapeDtypeStruct((count, hidden), BF16),
            jax.ShapeDtypeStruct((count, model), BF16),
            jax.ShapeDtypeStruct((edge, model), BF16),
            jax.ShapeDtypeStruct((pack, model), BF16),
            jax.ShapeDtypeStruct((pack, model), BF16),
            jax.ShapeDtypeStruct(blocks, BF16),
            jax.ShapeDtypeStruct(blocks, BF16),
        ],
        compiler_params=pltpu.CompilerParams(vmem_limit_bytes=GRANT << 20),
        cost_estimate=cost(20 << 30, 36 << 20),
        name="main",
    )(
        core, lat, before, after, left, right, *[weight.reshape(4, 4, model, width)] * 2,
        tokens, cot, a_own, w_in, w_out,
    )


def tail_body(
    tokens, act, w_out, cot_hbm, edge, before, after, weight, united, out,
    cot, planes, sem,
):
    step = pl.program_id(0)
    fine_rows, fine_cols, model = cot.shape
    cols = fine_cols // 2
    rows = fine_rows // 2
    copy = pltpu.make_async_copy(cot_hbm, cot, sem.at[0])

    @pl.when(step == 0)
    def _():
        copy.start()

    @pl.when(step < 4)
    def _():
        united[...] = (tokens[...].astype(F32) + dot_nn(act[...], w_out[...])).astype(BF16)

    @pl.when(step == 4)
    def _():
        copy.wait()
        r, c = iota((fine_cols, fine_cols), 0), iota((fine_cols, fine_cols), 1)
        pick = (c == 2 * (r % cols) + r // cols).astype(F32).astype(BF16)
        sides, above, below = [ref.astype(F32) for ref in (
            edge[...], before[fine_cols:], after[fine_cols:]
        )]
        place = iota((cols, model), 0)
        for e in range(fine_rows + 2):
            if e == 0:
                row, left, right = before[0:fine_cols], above[8:9], above[24:25]
            elif e == fine_rows + 1:
                row, left, right = after[0:fine_cols], below[0:1], below[16:17]
            else:
                at = e // 2 + 16 * (e % 2)
                row, left, right = cot[e - 1], sides[at : at + 1], sides[at + 32 : at + 33]
            found = dot_nn(pick, row)
            even, odd = found[:cols], found[cols:]
            taps = (
                jnp.where(place == 0, left, pltpu.roll(odd, 1, 0)),
                even,
                odd,
                jnp.where(place == cols - 1, right, pltpu.roll(even, cols - 1, 0)),
            )
            for tap in range(4):
                planes[e % 2, e // 2, :, tap * model : (tap + 1) * model] = taps[tap].astype(BF16)

    @pl.when(step >= 4)
    def _():
        k = step - 4
        source = planes[k % 2, pl.ds(k // 2, rows)].reshape(rows * cols, 4 * model)
        term = dot_nn(source, weight[0])

        @pl.when(k == 0)
        def _():
            out[...] = term

        @pl.when(k != 0)
        def _():
            out[...] += term


def tail_kernel(tokens, act, w_out, cot, edge, before, after, weight):
    fine_rows, fine_cols, model = cot.shape
    width = weight.shape[1]
    count, hidden = act.shape
    block = count // 4
    whole = lambda a: pl.BlockSpec(a.shape, lambda i: (0,) * a.ndim)
    size = fine_rows * fine_cols // 4
    tokens_of = lambda w: pl.BlockSpec((block, w), lambda i: (jnp.minimum(i, 3), 0))
    return pl.pallas_call(
        tail_body,
        grid=(8,),
        in_specs=[
            tokens_of(model),
            tokens_of(hidden),
            whole(w_out),
            pl.BlockSpec(memory_space=pl.ANY),
            whole(edge),
            whole(before),
            whole(after),
            pl.BlockSpec((1, 4 * model, width), lambda i: (jnp.maximum(i - 4, 0), 0, 0)),
        ],
        out_specs=[tokens_of(model), pl.BlockSpec((size, width), lambda i: (0, 0))],
        out_shape=[
            jax.ShapeDtypeStruct((count, model), BF16),
            jax.ShapeDtypeStruct((size, width), F32),
        ],
        scratch_shapes=[
            pltpu.VMEM((fine_rows, fine_cols, model), BF16),
            pltpu.VMEM((2, fine_rows // 2 + 1, fine_cols // 2, 4 * model), BF16),
            pltpu.SemaphoreType.DMA((1,)),
        ],
        compiler_params=pltpu.CompilerParams(vmem_limit_bytes=58 << 20),
        cost_estimate=cost(7 << 30, 22 << 20),
        name="tail",
    )(tokens, act, w_out, cot, edge, before, after, weight.reshape(4, 4 * model, width))


def sum_body(parts, in_grad, out_grad):
    total = parts[0].astype(F32)
    for i in range(1, parts.shape[0]):
        total = total + parts[i].astype(F32)
    in_grad[...] = total[:64]
    packed = total[64:]
    out_grad[...] = jnp.concatenate(
        [packed, pltpu.roll(packed, 64, 1)], axis=0
    ).T[:64, :]


def sum_blocks(parts):
    return pl.pallas_call(
        sum_body,
        out_shape=[
            jax.ShapeDtypeStruct((64, 128), F32),
            jax.ShapeDtypeStruct((64, 64), F32),
        ],
        compiler_params=pltpu.CompilerParams(vmem_limit_bytes=8 << 20),
        cost_estimate=cost(1 << 20, 2 << 20),
        name="sum_blocks",
    )(parts)


def swap(last, first, axis, wrap):
    devices = lax.axis_size(axis)
    up = [(i, (i + 1) % devices) for i in range(devices if wrap else devices - 1)]
    down = [(j, i) for i, j in up]
    one = lax.ppermute(last, axis, up)
    other = lax.ppermute(first, axis, down)
    return one, other


def halos(latents, tokens, cot):
    before, after = swap(latents[-1], latents[0], "lat", False)

    def column(c):
        place = c % latents.shape[1]
        ends = [a[place : place + 1] for a in (before, after)]
        parts = [ends[0], latents[:, c], ends[1], jnp.zeros((6, latents.shape[2]), BF16)]
        for fine in (tokens, cot):
            parts.append(jnp.pad(fine[1::2, c], ((1, 7), (0, 0))))
            parts.append(jnp.pad(fine[0::2, c], ((0, 8), (0, 0))))
        return jnp.concatenate(parts, axis=0)

    left, right = swap(column(-1), column(0), "lon", True)
    return before, after, left, right


def chip_groups():
    return [
        [
            (x * 2 + y_lo) * 16 + z * 4 + y_hi * 2 + core
            for z in range(4)
            for x in range(4)
            for y_hi in range(2)
            for y_lo in range(2)
        ]
        for core in range(2)
    ]


def other_core(array):
    return lax.ppermute(array, "lon", [(i, i ^ 1) for i in range(16)])


def shards(fine_tokens, latents, upsample_weight, uniting_in, uniting_out, cotangent):
    count = fine_tokens.shape[0] * fine_tokens.shape[1]
    model = fine_tokens.shape[2]
    core = (lax.axis_index("lon") % 2).astype(jnp.int32).reshape(1)
    tokens = fine_tokens.reshape(count, model)
    cot = cotangent.reshape(count, model)

    before, after, left, right = halos(latents, fine_tokens, cotangent)
    a_own = dot_nt(cot, uniting_out).astype(BF16)
    act, up_cot, up_cot_edge, first_row, last_row, keep, send = main_kernel(
        core, latents, before, after, left, right, upsample_weight,
        tokens, cot, a_own, uniting_in, uniting_out,
    )
    other = other_core(send)
    above, below = swap(last_row, first_row, "lat", False)
    halves = (keep.astype(F32) + other.astype(F32)).astype(BF16).reshape(64, 96, 128)
    parts = lax.all_to_all(
        halves, BOTH, 0, 0, axis_index_groups=chip_groups(), tiled=True
    )
    united, latent_grad = tail_kernel(
        tokens, act, uniting_out, up_cot.reshape(fine_tokens.shape), up_cot_edge,
        above, below, upsample_weight,
    )
    in_grad, out_grad = sum_blocks(parts)
    return (
        united.reshape(fine_tokens.shape),
        latent_grad.reshape(latents.shape),
        in_grad,
        out_grad,
    )


def solution(mesh):
    return jax.shard_map(
        shards,
        mesh=mesh,
        in_specs=(
            P("lat", "lon", None),
            P("lat", "lon", None),
            P(),
            P(),
            P(),
            P("lat", "lon", None),
        ),
        out_specs=(P("lat", "lon", None), P("lat", "lon", None), P("lon", "lat"), P("lon", "lat")),
        check_vma=False,
    )
```

```python
import jax
import jax.numpy as jnp
from jax import lax
from jax.experimental import pallas as pl
from jax.experimental.pallas import tpu as pltpu
from jax.sharding import PartitionSpec as P

BF16 = jnp.bfloat16
F32 = jnp.float32
BOTH = ("lat", "lon")
GRANT = 44
WINDOW = 57
FLOPS = 4


def dot_nn(a, b):
    return lax.dot_general(a, b, (((1,), (0,)), ((), ())), preferred_element_type=F32)


def dot_nt(a, b):
    return lax.dot_general(a, b, (((1,), (1,)), ((), ())), preferred_element_type=F32)


def cost(flops, nbytes):
    return pl.CostEstimate(flops=flops, bytes_accessed=nbytes, transcendentals=0)


def iota(shape, dim):
    return lax.broadcasted_iota(jnp.int32, shape, dim)


def main_body(
    core, lat, before, after, left, right, w_a, w_b, tokens, cot, a_own, w_in_hbm, w_out_hbm,
    act_out, up_cot, up_cot_edge, first_row, last_row, keep, send,
    sources, edges, tokens_edge, cot_edge, w_in, w_out, up, act, pre, pre_edge,
    turned, sems,
):
    step = pl.program_id(0)
    rows, cols, width = lat.shape
    hidden, model = w_out.shape
    half_model = model // 2
    block = up_cot.shape[0]
    count = act.shape[0]
    fine_cols = 2 * cols
    copies = [
        pltpu.make_async_copy(source, target, sems.at[i])
        for i, (source, target) in enumerate(
            ((w_in_hbm, w_in), (w_out_hbm, w_out))
        )
    ]

    act_copy = pltpu.make_async_copy(act, act_out, sems.at[2])

    @pl.when(step == 1)
    def _():
        for copy in copies:
            copy.start()

    @pl.when(step == 9)
    def _():
        act_copy.start()

    @pl.when(step == 0)
    def _():
        lefts, rights = left[0:16].astype(F32), right[0:16].astype(F32)
        edges[...] = jnp.zeros_like(edges)
        place = iota((cols, width), 0)
        for r in range(rows + 2):
            row = before[0:cols] if r == 0 else after[0:cols] if r == rows + 1 else lat[r - 1]
            wide = row.astype(F32)
            at = slice(16 + r * cols, 16 + (r + 1) * cols)
            sources[0, at] = row
            sources[1, at] = jnp.where(
                place == 0, lefts[r : r + 1], pltpu.roll(wide, 1, 0)
            ).astype(BF16)
            sources[2, at] = jnp.where(
                place == cols - 1, rights[r : r + 1], pltpu.roll(wide, cols - 1, 0)
            ).astype(BF16)
            sources[3, at] = row
            edges[0, r : r + 1] = wide[cols - 1 : cols]
            edges[1, r : r + 1] = wide[0:1]
        last = 16 + (rows + 2) * cols
        for i, edge in enumerate((rights, edges[0], edges[1], lefts)):
            sources[i, 0:16] = edge.astype(BF16)
            sources[i, last : last + 16] = pltpu.roll(edge, 15, 0).astype(BF16)
        for ref, part in ((tokens_edge, 16), (cot_edge, 48)):
            ref[0:32] = left[part : part + 32]
            ref[32:] = right[part : part + 32]

    @pl.when(step < 4)
    def _():
        parity, half = step // 2, step % 2
        size = (rows + 1) * cols
        planes = []
        for q, taps in enumerate((((1, 0), (3, 1)), ((0, 2), (2, 3)))):
            total_a = total_b = None
            for tap, i in taps:
                term_a = dot_nt(sources[i, 16 + cols : 32 + cols + size], w_a[0, tap])
                term_b = dot_nt(sources[i, 0 : 16 + size], w_b[0, tap])
                total_a = term_a if total_a is None else total_a + term_a
                total_b = term_b if total_b is None else total_b + term_b
            planes.append((total_a[:size] + total_b[16:]).astype(BF16))
            side = (total_a[size:] + total_b[:16]).astype(BF16)
            at = count + fine_cols + (1 - q) * 32 + (1 - parity) * 16
            up[half, pl.ds(pl.multiple_of(at, 16), 16)] = side
        r, k = iota((fine_cols, fine_cols), 0), iota((fine_cols, fine_cols), 1)
        spread = (k == (r % 2) * cols + r // 2).astype(F32).astype(BF16)
        for m in range(rows + 1):
            pair = jnp.concatenate([z[m * cols : (m + 1) * cols] for z in planes], axis=0)
            value = dot_nn(spread, pair).astype(BF16)
            even = 2 * m * fine_cols if m < rows else count
            odd = (2 * m - 1) * fine_cols if m > 0 else count
            at = even + parity * (odd - even)
            up[half, pl.ds(pl.multiple_of(at, 128), fine_cols)] = value

    @pl.when(step == 4)
    def _():
        for copy in copies:
            copy.wait()

    def network(tokens_of, up_of, a_of, span):
        h = dot_nn(tokens_of(), w_in[:model, span])
        h += dot_nn(up_of(0), w_in[model : model + half_model, span])
        h += dot_nn(up_of(1), w_in[model + half_model :, span])
        g = 0.5 * jnp.tanh(0.5 * h) + 0.5
        y = h * g
        a = a_of()
        return y.astype(BF16), (a * (g + y * (1.0 - g))).astype(BF16)

    @pl.when(step == 4)
    def _():
        for n in range(0, hidden, 256):
            span = slice(n, n + 256)
            _, pre_edge[:, span] = network(
                lambda: tokens_edge[...],
                lambda i: up[i, count + fine_cols :],
                lambda: dot_nt(cot_edge[...], w_out[span, :]),
                span,
            )
        value = dot_nt(pre_edge[...], w_in[model:, :]).astype(BF16)
        up_cot_edge[...] = value
        for i in range(2):
            at = slice(fine_cols + 16 * i, fine_cols + 16 * i + 16)
            last_row[at] = value[32 * i : 32 * i + 16]
            first_row[at] = value[32 * i + 16 : 32 * i + 32]

    @pl.when((step > 4) & (step < 9))
    def _():
        at = pl.ds(pl.multiple_of((step - 5) * block, block), block)
        for n in range(0, hidden, 256):
            span = slice(n, n + 256)
            wide, grad = network(
                lambda: tokens[...],
                lambda i: up[i, at],
                lambda: a_own[:, span].astype(F32),
                span,
            )
            act[at, span] = wide
            pre[at, span] = grad
        turned[0:model, at] = tokens[...].T
        turned[model : model + half_model, at] = up[0, at].T
        turned[model + half_model : 2 * model, at] = up[1, at].T
        turned[2 * model :, at] = cot[...].T
        up_cot[...] = dot_nt(pre[at, :], w_in[model:, :]).astype(BF16)

    @pl.when(step == 5)
    def _():
        first_row[0:fine_cols] = up_cot[0:fine_cols]

    @pl.when(step == 8)
    def _():
        last_row[0:fine_cols] = up_cot[block - fine_cols :]

    for j in range(4):

        @pl.when(step == 9 + j)
        def _():
            span = slice(j * 256, (j + 1) * 256)
            mine = core[0]
            total = dot_nn(turned[: 2 * model], pre[:, span])
            for z in range(4):
                for y_hi in range(2):
                    base = (z * 2 + y_hi) * 128
                    first, second = total[base : base + 64], total[base + 64 : base + 128]
                    own = jnp.where(mine == 0, first, second).astype(BF16)
                    other = jnp.where(mine == 0, second, first).astype(BF16)
                    for y_lo in range(2):
                        lanes = slice(y_lo * 128, (y_lo + 1) * 128)
                        keep[z, j, y_hi * 2 + y_lo, 0:64] = own[:, lanes]
                        send[z, j, y_hi * 2 + y_lo, 0:64] = other[:, lanes]
            total = dot_nn(turned[2 * model :], act[:, span])
            low = iota((32, 128), 1) < 64
            for lat_id in range(8):
                for y_hi in range(2):
                    lanes = slice(y_hi * 128, (y_hi + 1) * 128)
                    a = total[lat_id * 64 : lat_id * 64 + 32, lanes]
                    b = total[lat_id * 64 + 32 : lat_id * 64 + 64, lanes]
                    first = jnp.where(low, a, pltpu.roll(b, 64, 1))
                    second = jnp.where(low, pltpu.roll(a, 64, 1), b)
                    at = y_hi * 2 + lat_id % 2
                    keep[j, lat_id // 2, at, 64:96] = jnp.where(
                        mine == 0, first, second
                    ).astype(BF16)
                    send[j, lat_id // 2, at, 64:96] = jnp.where(
                        mine == 0, second, first
                    ).astype(BF16)

    @pl.when(step == 12)
    def _():
        act_copy.wait()


def project_body(cot, w_out, out):
    out[...] = dot_nt(cot[...], w_out[...]).astype(BF16)


def project(cot, w_out):
    count, model = cot.shape
    hidden = w_out.shape[0]
    block = count // 4
    return pl.pallas_call(
        project_body,
        grid=(4,),
        in_specs=[
            pl.BlockSpec((block, model), lambda i: (i, 0)),
            pl.BlockSpec((hidden, model), lambda i: (0, 0), pipeline_mode=pl.Buffered(1)),
        ],
        out_specs=pl.BlockSpec((block, hidden), lambda i: (i, 0)),
        out_shape=jax.ShapeDtypeStruct((count, hidden), BF16),
        compiler_params=pltpu.CompilerParams(vmem_limit_bytes=WINDOW << 20),
        cost_estimate=cost(FLOPS << 30, 7 << 20),
        name="project",
    )(cot, w_out)


def main_kernel(core, lat, before, after, left, right, weight, tokens, cot, a_own, w_in, w_out):
    rows, cols, width = lat.shape
    model = weight.shape[0] // 16
    half = model // 2
    count = tokens.shape[0]
    hidden = w_out.shape[0]
    block = count // 4
    edge = 64
    pack = 2 * cols + 32
    clamp = lambda i, low: jnp.clip(i - low, 0, 3)
    whole = lambda *shape: pl.BlockSpec(
        shape, lambda i, c: (0,) * len(shape), pipeline_mode=pl.Buffered(1)
    )
    kernel_row = lambda i, top: (top - clamp(i, 0) // 2, 0, clamp(i, 0) % 2, 0)
    tokens_of = lambda w: pl.BlockSpec((block, w), lambda i, c: (clamp(i, 5), 0))
    blocks = (4, 4, 4, 96, 128)
    return pl.pallas_call(
        main_body,
        grid_spec=pltpu.PrefetchScalarGridSpec(
            num_scalar_prefetch=1,
            grid=(13,),
            in_specs=[
                whole(rows, cols, width),
                whole(*before.shape),
                whole(*after.shape),
                whole(*left.shape),
                whole(*right.shape),
                pl.BlockSpec((1, 4, half, width), lambda i, c: kernel_row(i, 1)),
                pl.BlockSpec((1, 4, half, width), lambda i, c: kernel_row(i, 3)),
                tokens_of(model),
                tokens_of(model),
                tokens_of(hidden),
                pl.BlockSpec(memory_space=pltpu.HBM),
                pl.BlockSpec(memory_space=pltpu.HBM),
            ],
            out_specs=[
                pl.BlockSpec(memory_space=pl.ANY),
                tokens_of(model),
                whole(edge, model),
                whole(pack, model),
                whole(pack, model),
                whole(*blocks),
                whole(*blocks),
            ],
            scratch_shapes=[
                pltpu.VMEM((4, (rows + 2) * cols + 32, width), BF16),
                pltpu.VMEM((2, 16, width), F32),
                pltpu.VMEM((edge, model), BF16),
                pltpu.VMEM((edge, model), BF16),
                pltpu.VMEM((2 * model, hidden), BF16),
                pltpu.VMEM((hidden, model), BF16),
                pltpu.VMEM((2, count + 2 * cols + edge, half), BF16),
                pltpu.VMEM((count, hidden), BF16),
                pltpu.VMEM((count, hidden), BF16),
                pltpu.VMEM((edge, hidden), BF16),
                pltpu.VMEM((3 * model, count), BF16),
                pltpu.SemaphoreType.DMA((3,)),
            ],
        ),
        out_shape=[
            jax.ShapeDtypeStruct((count, hidden), BF16),
            jax.ShapeDtypeStruct((count, model), BF16),
            jax.ShapeDtypeStruct((edge, model), BF16),
            jax.ShapeDtypeStruct((pack, model), BF16),
            jax.ShapeDtypeStruct((pack, model), BF16),
            jax.ShapeDtypeStruct(blocks, BF16),
            jax.ShapeDtypeStruct(blocks, BF16),
        ],
        compiler_params=pltpu.CompilerParams(vmem_limit_bytes=GRANT << 20),
        cost_estimate=cost(20 << 30, 36 << 20),
        name="main",
    )(
        core, lat, before, after, left, right, *[weight.reshape(4, 4, model, width)] * 2,
        tokens, cot, a_own, w_in, w_out,
    )


def tail_body(
    tokens, act, w_out, cot_hbm, edge, before, after, weight, united, out,
    cot, planes, sem,
):
    step = pl.program_id(0)
    fine_rows, fine_cols, model = cot.shape
    cols = fine_cols // 2
    rows = fine_rows // 2
    copy = pltpu.make_async_copy(cot_hbm, cot, sem.at[0])

    @pl.when(step == 0)
    def _():
        copy.start()

    @pl.when(step < 4)
    def _():
        united[...] = (tokens[...].astype(F32) + dot_nn(act[...], w_out[...])).astype(BF16)

    @pl.when(step == 4)
    def _():
        copy.wait()
        r, c = iota((fine_cols, fine_cols), 0), iota((fine_cols, fine_cols), 1)
        pick = (c == 2 * (r % cols) + r // cols).astype(F32).astype(BF16)
        sides, above, below = [ref.astype(F32) for ref in (
            edge[...], before[fine_cols:], after[fine_cols:]
        )]
        place = iota((cols, model), 0)
        for e in range(fine_rows + 2):
            if e == 0:
                row, left, right = before[0:fine_cols], above[8:9], above[24:25]
            elif e == fine_rows + 1:
                row, left, right = after[0:fine_cols], below[0:1], below[16:17]
            else:
                at = e // 2 + 16 * (e % 2)
                row, left, right = cot[e - 1], sides[at : at + 1], sides[at + 32 : at + 33]
            found = dot_nn(pick, row)
            even, odd = found[:cols], found[cols:]
            taps = (
                jnp.where(place == 0, left, pltpu.roll(odd, 1, 0)),
                even,
                odd,
                jnp.where(place == cols - 1, right, pltpu.roll(even, cols - 1, 0)),
            )
            for tap in range(4):
                planes[e % 2, e // 2, :, tap * model : (tap + 1) * model] = taps[tap].astype(BF16)

    @pl.when(step >= 4)
    def _():
        k = step - 4
        source = planes[k % 2, pl.ds(k // 2, rows)].reshape(rows * cols, 4 * model)
        term = dot_nn(source, weight[0])

        @pl.when(k == 0)
        def _():
            out[...] = term

        @pl.when(k != 0)
        def _():
            out[...] += term


def tail_kernel(tokens, act, w_out, cot, edge, before, after, weight):
    fine_rows, fine_cols, model = cot.shape
    width = weight.shape[1]
    count, hidden = act.shape
    block = count // 4
    whole = lambda a: pl.BlockSpec(a.shape, lambda i: (0,) * a.ndim)
    size = fine_rows * fine_cols // 4
    tokens_of = lambda w: pl.BlockSpec((block, w), lambda i: (jnp.minimum(i, 3), 0))
    return pl.pallas_call(
        tail_body,
        grid=(8,),
        in_specs=[
            tokens_of(model),
            tokens_of(hidden),
            whole(w_out),
            pl.BlockSpec(memory_space=pl.ANY),
            whole(edge),
            whole(before),
            whole(after),
            pl.BlockSpec((1, 4 * model, width), lambda i: (jnp.maximum(i - 4, 0), 0, 0)),
        ],
        out_specs=[tokens_of(model), pl.BlockSpec((size, width), lambda i: (0, 0))],
        out_shape=[
            jax.ShapeDtypeStruct((count, model), BF16),
            jax.ShapeDtypeStruct((size, width), F32),
        ],
        scratch_shapes=[
            pltpu.VMEM((fine_rows, fine_cols, model), BF16),
            pltpu.VMEM((2, fine_rows // 2 + 1, fine_cols // 2, 4 * model), BF16),
            pltpu.SemaphoreType.DMA((1,)),
        ],
        compiler_params=pltpu.CompilerParams(vmem_limit_bytes=58 << 20),
        cost_estimate=cost(7 << 30, 22 << 20),
        name="tail",
    )(tokens, act, w_out, cot, edge, before, after, weight.reshape(4, 4 * model, width))


def sum_body(parts, in_grad, out_grad):
    total = parts[0].astype(F32)
    for i in range(1, parts.shape[0]):
        total = total + parts[i].astype(F32)
    in_grad[...] = total[:64]
    packed = total[64:]
    out_grad[...] = jnp.concatenate(
        [packed, pltpu.roll(packed, 64, 1)], axis=0
    ).T[:64, :]


def sum_blocks(parts):
    return pl.pallas_call(
        sum_body,
        out_shape=[
            jax.ShapeDtypeStruct((64, 128), F32),
            jax.ShapeDtypeStruct((64, 64), F32),
        ],
        compiler_params=pltpu.CompilerParams(vmem_limit_bytes=8 << 20),
        cost_estimate=cost(1 << 20, 2 << 20),
        name="sum_blocks",
    )(parts)


def swap(last, first, axis, wrap):
    devices = lax.axis_size(axis)
    up = [(i, (i + 1) % devices) for i in range(devices if wrap else devices - 1)]
    down = [(j, i) for i, j in up]
    one = lax.ppermute(last, axis, up)
    other = lax.ppermute(first, axis, down)
    return one, other


def halos(latents, tokens, cot):
    before, after = swap(latents[-1], latents[0], "lat", False)

    def column(c):
        place = c % latents.shape[1]
        ends = [a[place : place + 1] for a in (before, after)]
        parts = [ends[0], latents[:, c], ends[1], jnp.zeros((6, latents.shape[2]), BF16)]
        for fine in (tokens, cot):
            parts.append(jnp.pad(fine[1::2, c], ((1, 7), (0, 0))))
            parts.append(jnp.pad(fine[0::2, c], ((0, 8), (0, 0))))
        return jnp.concatenate(parts, axis=0)

    left, right = swap(column(-1), column(0), "lon", True)
    return before, after, left, right


def chip_groups():
    return [
        [
            (x * 2 + y_lo) * 16 + z * 4 + y_hi * 2 + core
            for z in range(4)
            for x in range(4)
            for y_hi in range(2)
            for y_lo in range(2)
        ]
        for core in range(2)
    ]


def other_core(array):
    return lax.ppermute(array, "lon", [(i, i ^ 1) for i in range(16)])


def shards(fine_tokens, latents, upsample_weight, uniting_in, uniting_out, cotangent):
    count = fine_tokens.shape[0] * fine_tokens.shape[1]
    model = fine_tokens.shape[2]
    core = (lax.axis_index("lon") % 2).astype(jnp.int32).reshape(1)
    tokens = fine_tokens.reshape(count, model)
    cot = cotangent.reshape(count, model)

    before, after, left, right = halos(latents, fine_tokens, cotangent)
    a_own = project(cot, uniting_out)
    act, up_cot, up_cot_edge, first_row, last_row, keep, send = main_kernel(
        core, latents, before, after, left, right, upsample_weight,
        tokens, cot, a_own, uniting_in, uniting_out,
    )
    other = other_core(send)
    above, below = swap(last_row, first_row, "lat", False)
    halves = (keep.astype(F32) + other.astype(F32)).astype(BF16).reshape(64, 96, 128)
    parts = lax.all_to_all(
        halves, BOTH, 0, 0, axis_index_groups=chip_groups(), tiled=True
    )
    united, latent_grad = tail_kernel(
        tokens, act, uniting_out, up_cot.reshape(fine_tokens.shape), up_cot_edge,
        above, below, upsample_weight,
    )
    in_grad, out_grad = sum_blocks(parts)
    return (
        united.reshape(fine_tokens.shape),
        latent_grad.reshape(latents.shape),
        in_grad,
        out_grad,
    )


def solution(mesh):
    return jax.shard_map(
        shards,
        mesh=mesh,
        in_specs=(
            P("lat", "lon", None),
            P("lat", "lon", None),
            P(),
            P(),
            P(),
            P("lat", "lon", None),
        ),
        out_specs=(P("lat", "lon", None), P("lat", "lon", None), P("lon", "lat"), P("lon", "lat")),
        check_vma=False,
    )
```

```python
import jax
import jax.numpy as jnp
from jax import lax
from jax.experimental import pallas as pl
from jax.experimental.pallas import tpu as pltpu
from jax.sharding import PartitionSpec as P

BF16 = jnp.bfloat16
F32 = jnp.float32
BOTH = ("lat", "lon")
GRANT = 46


def dot_nn(a, b):
    return lax.dot_general(a, b, (((1,), (0,)), ((), ())), preferred_element_type=F32)


def dot_nt(a, b):
    return lax.dot_general(a, b, (((1,), (1,)), ((), ())), preferred_element_type=F32)


def cost(flops, nbytes):
    return pl.CostEstimate(flops=flops, bytes_accessed=nbytes, transcendentals=0)


def iota(shape, dim):
    return lax.broadcasted_iota(jnp.int32, shape, dim)


def main_body(
    core, lat, before, after, left, right, w_a, w_b, tokens, cot, a_own, w_in_hbm, w_out_hbm,
    act_out, up_cot, up_cot_edge, first_row, last_row, keep, send,
    sources, edges, tokens_edge, cot_edge, w_in, w_out, up, act, pre, pre_edge,
    turned, sems,
):
    step = pl.program_id(0)
    rows, cols, width = lat.shape
    hidden, model = w_out.shape
    half_model = model // 2
    block = up_cot.shape[0]
    count = act.shape[0]
    fine_cols = 2 * cols
    copies = [
        pltpu.make_async_copy(source, target, sems.at[i])
        for i, (source, target) in enumerate(
            ((w_in_hbm, w_in), (w_out_hbm, w_out))
        )
    ]

    act_copy = pltpu.make_async_copy(act, act_out, sems.at[2])

    @pl.when(step == 1)
    def _():
        for copy in copies:
            copy.start()

    @pl.when(step == 9)
    def _():
        act_copy.start()

    @pl.when(step == 0)
    def _():
        lefts, rights = left[0:16].astype(F32), right[0:16].astype(F32)
        edges[...] = jnp.zeros_like(edges)
        place = iota((cols, width), 0)
        for r in range(rows + 2):
            row = before[0:cols] if r == 0 else after[0:cols] if r == rows + 1 else lat[r - 1]
            wide = row.astype(F32)
            at = slice(16 + r * cols, 16 + (r + 1) * cols)
            sources[0, at] = row
            sources[1, at] = jnp.where(
                place == 0, lefts[r : r + 1], pltpu.roll(wide, 1, 0)
            ).astype(BF16)
            sources[2, at] = jnp.where(
                place == cols - 1, rights[r : r + 1], pltpu.roll(wide, cols - 1, 0)
            ).astype(BF16)
            sources[3, at] = row
            edges[0, r : r + 1] = wide[cols - 1 : cols]
            edges[1, r : r + 1] = wide[0:1]
        last = 16 + (rows + 2) * cols
        for i, edge in enumerate((rights, edges[0], edges[1], lefts)):
            sources[i, 0:16] = edge.astype(BF16)
            sources[i, last : last + 16] = pltpu.roll(edge, 15, 0).astype(BF16)
        for ref, part in ((tokens_edge, 16), (cot_edge, 48)):
            ref[0:32] = left[part : part + 32]
            ref[32:] = right[part : part + 32]

    @pl.when(step < 4)
    def _():
        parity, half = step // 2, step % 2
        size = (rows + 1) * cols
        planes = []
        for q, taps in enumerate((((1, 0), (3, 1)), ((0, 2), (2, 3)))):
            total_a = total_b = None
            for tap, i in taps:
                term_a = dot_nt(sources[i, 16 + cols : 32 + cols + size], w_a[0, tap])
                term_b = dot_nt(sources[i, 0 : 16 + size], w_b[0, tap])
                total_a = term_a if total_a is None else total_a + term_a
                total_b = term_b if total_b is None else total_b + term_b
            planes.append((total_a[:size] + total_b[16:]).astype(BF16))
            side = (total_a[size:] + total_b[:16]).astype(BF16)
            at = count + fine_cols + (1 - q) * 32 + (1 - parity) * 16
            up[half, pl.ds(pl.multiple_of(at, 16), 16)] = side
        r, k = iota((fine_cols, fine_cols), 0), iota((fine_cols, fine_cols), 1)
        spread = (k == (r % 2) * cols + r // 2).astype(F32).astype(BF16)
        for m in range(rows + 1):
            pair = jnp.concatenate([z[m * cols : (m + 1) * cols] for z in planes], axis=0)
            value = dot_nn(spread, pair).astype(BF16)
            even = 2 * m * fine_cols if m < rows else count
            odd = (2 * m - 1) * fine_cols if m > 0 else count
            at = even + parity * (odd - even)
            up[half, pl.ds(pl.multiple_of(at, 128), fine_cols)] = value

    @pl.when(step == 4)
    def _():
        for copy in copies:
            copy.wait()

    def network(tokens_of, up_of, a_of, span):
        h = dot_nn(tokens_of(), w_in[:model, span])
        h += dot_nn(up_of(0), w_in[model : model + half_model, span])
        h += dot_nn(up_of(1), w_in[model + half_model :, span])
        g = 0.5 * jnp.tanh(0.5 * h) + 0.5
        y = h * g
        a = a_of()
        return y.astype(BF16), (a * (g + y * (1.0 - g))).astype(BF16)

    @pl.when(step == 4)
    def _():
        for n in range(0, hidden, 256):
            span = slice(n, n + 256)
            _, pre_edge[:, span] = network(
                lambda: tokens_edge[...],
                lambda i: up[i, count + fine_cols :],
                lambda: dot_nt(cot_edge[...], w_out[span, :]),
                span,
            )
        value = dot_nt(pre_edge[...], w_in[model:, :]).astype(BF16)
        up_cot_edge[...] = value
        for i in range(2):
            at = slice(fine_cols + 16 * i, fine_cols + 16 * i + 16)
            last_row[at] = value[32 * i : 32 * i + 16]
            first_row[at] = value[32 * i + 16 : 32 * i + 32]

    def own_tokens(a_of):
        at = pl.ds(pl.multiple_of((step - 5) * block, block), block)
        for n in range(0, hidden, 256):
            span = slice(n, n + 256)
            wide, grad = network(
                lambda: tokens[...],
                lambda i: up[i, at],
                lambda: a_of(span),
                span,
            )
            act[at, span] = wide
            pre[at, span] = grad
        turned[0:model, at] = tokens[...].T
        turned[model : model + half_model, at] = up[0, at].T
        turned[model + half_model : 2 * model, at] = up[1, at].T
        turned[2 * model :, at] = cot[...].T
        up_cot[...] = dot_nt(pre[at, :], w_in[model:, :]).astype(BF16)

    @pl.when((step > 4) & (step < 7))
    def _():
        own_tokens(lambda span: a_own[:, span].astype(F32))

    @pl.when((step > 6) & (step < 9))
    def _():
        own_tokens(lambda span: dot_nt(cot[...], w_out[span, :]))

    @pl.when(step == 5)
    def _():
        first_row[0:fine_cols] = up_cot[0:fine_cols]

    @pl.when(step == 8)
    def _():
        last_row[0:fine_cols] = up_cot[block - fine_cols :]

    for j in range(4):

        @pl.when(step == 9 + j)
        def _():
            span = slice(j * 256, (j + 1) * 256)
            mine = core[0]
            total = dot_nn(turned[: 2 * model], pre[:, span])
            for z in range(4):
                for y_hi in range(2):
                    base = (z * 2 + y_hi) * 128
                    first, second = total[base : base + 64], total[base + 64 : base + 128]
                    own = jnp.where(mine == 0, first, second).astype(BF16)
                    other = jnp.where(mine == 0, second, first).astype(BF16)
                    for y_lo in range(2):
                        lanes = slice(y_lo * 128, (y_lo + 1) * 128)
                        keep[z, j, y_hi * 2 + y_lo, 0:64] = own[:, lanes]
                        send[z, j, y_hi * 2 + y_lo, 0:64] = other[:, lanes]
            total = dot_nn(turned[2 * model :], act[:, span])
            low = iota((32, 128), 1) < 64
            for lat_id in range(8):
                for y_hi in range(2):
                    lanes = slice(y_hi * 128, (y_hi + 1) * 128)
                    a = total[lat_id * 64 : lat_id * 64 + 32, lanes]
                    b = total[lat_id * 64 + 32 : lat_id * 64 + 64, lanes]
                    first = jnp.where(low, a, pltpu.roll(b, 64, 1))
                    second = jnp.where(low, pltpu.roll(a, 64, 1), b)
                    at = y_hi * 2 + lat_id % 2
                    keep[j, lat_id // 2, at, 64:96] = jnp.where(
                        mine == 0, first, second
                    ).astype(BF16)
                    send[j, lat_id // 2, at, 64:96] = jnp.where(
                        mine == 0, second, first
                    ).astype(BF16)

    @pl.when(step == 12)
    def _():
        act_copy.wait()


def main_kernel(core, lat, before, after, left, right, weight, tokens, cot, a_own, w_in, w_out):
    rows, cols, width = lat.shape
    model = weight.shape[0] // 16
    half = model // 2
    count = tokens.shape[0]
    hidden = w_out.shape[0]
    block = count // 4
    edge = 64
    pack = 2 * cols + 32
    clamp = lambda i, low: jnp.clip(i - low, 0, 3)
    whole = lambda *shape: pl.BlockSpec(shape, lambda i, c: (0,) * len(shape))
    kernel_row = lambda i, top: (top - clamp(i, 0) // 2, 0, clamp(i, 0) % 2, 0)
    tokens_of = lambda w: pl.BlockSpec((block, w), lambda i, c: (clamp(i, 5), 0))
    blocks = (4, 4, 4, 96, 128)
    return pl.pallas_call(
        main_body,
        grid_spec=pltpu.PrefetchScalarGridSpec(
            num_scalar_prefetch=1,
            grid=(13,),
            in_specs=[
                whole(rows, cols, width),
                whole(*before.shape),
                whole(*after.shape),
                whole(*left.shape),
                whole(*right.shape),
                pl.BlockSpec((1, 4, half, width), lambda i, c: kernel_row(i, 1)),
                pl.BlockSpec((1, 4, half, width), lambda i, c: kernel_row(i, 3)),
                tokens_of(model),
                tokens_of(model),
                pl.BlockSpec((block, hidden), lambda i, c: (jnp.clip(i - 5, 0, 1), 0)),
                pl.BlockSpec(memory_space=pltpu.HBM),
                pl.BlockSpec(memory_space=pltpu.HBM),
            ],
            out_specs=[
                pl.BlockSpec(memory_space=pl.ANY),
                tokens_of(model),
                whole(edge, model),
                whole(pack, model),
                whole(pack, model),
                whole(*blocks),
                whole(*blocks),
            ],
            scratch_shapes=[
                pltpu.VMEM((4, (rows + 2) * cols + 32, width), BF16),
                pltpu.VMEM((2, 16, width), F32),
                pltpu.VMEM((edge, model), BF16),
                pltpu.VMEM((edge, model), BF16),
                pltpu.VMEM((2 * model, hidden), BF16),
                pltpu.VMEM((hidden, model), BF16),
                pltpu.VMEM((2, count + 2 * cols + edge, half), BF16),
                pltpu.VMEM((count, hidden), BF16),
                pltpu.VMEM((count, hidden), BF16),
                pltpu.VMEM((edge, hidden), BF16),
                pltpu.VMEM((3 * model, count), BF16),
                pltpu.SemaphoreType.DMA((3,)),
            ],
        ),
        out_shape=[
            jax.ShapeDtypeStruct((count, hidden), BF16),
            jax.ShapeDtypeStruct((count, model), BF16),
            jax.ShapeDtypeStruct((edge, model), BF16),
            jax.ShapeDtypeStruct((pack, model), BF16),
            jax.ShapeDtypeStruct((pack, model), BF16),
            jax.ShapeDtypeStruct(blocks, BF16),
            jax.ShapeDtypeStruct(blocks, BF16),
        ],
        compiler_params=pltpu.CompilerParams(vmem_limit_bytes=GRANT << 20),
        cost_estimate=cost(20 << 30, 36 << 20),
        name="main",
    )(
        core, lat, before, after, left, right, *[weight.reshape(4, 4, model, width)] * 2,
        tokens, cot, a_own, w_in, w_out,
    )


def tail_body(
    tokens, act, w_out, cot_hbm, edge, before, after, weight, united, out,
    cot, planes, sem,
):
    step = pl.program_id(0)
    fine_rows, fine_cols, model = cot.shape
    cols = fine_cols // 2
    rows = fine_rows // 2
    copy = pltpu.make_async_copy(cot_hbm, cot, sem.at[0])

    @pl.when(step == 0)
    def _():
        copy.start()

    @pl.when(step < 4)
    def _():
        united[...] = (tokens[...].astype(F32) + dot_nn(act[...], w_out[...])).astype(BF16)

    @pl.when(step == 4)
    def _():
        copy.wait()
        r, c = iota((fine_cols, fine_cols), 0), iota((fine_cols, fine_cols), 1)
        pick = (c == 2 * (r % cols) + r // cols).astype(F32).astype(BF16)
        sides, above, below = [ref.astype(F32) for ref in (
            edge[...], before[fine_cols:], after[fine_cols:]
        )]
        place = iota((cols, model), 0)
        for e in range(fine_rows + 2):
            if e == 0:
                row, left, right = before[0:fine_cols], above[8:9], above[24:25]
            elif e == fine_rows + 1:
                row, left, right = after[0:fine_cols], below[0:1], below[16:17]
            else:
                at = e // 2 + 16 * (e % 2)
                row, left, right = cot[e - 1], sides[at : at + 1], sides[at + 32 : at + 33]
            found = dot_nn(pick, row)
            even, odd = found[:cols], found[cols:]
            taps = (
                jnp.where(place == 0, left, pltpu.roll(odd, 1, 0)),
                even,
                odd,
                jnp.where(place == cols - 1, right, pltpu.roll(even, cols - 1, 0)),
            )
            for tap in range(4):
                planes[e % 2, e // 2, :, tap * model : (tap + 1) * model] = taps[tap].astype(BF16)

    @pl.when(step >= 4)
    def _():
        k = step - 4
        source = planes[k % 2, pl.ds(k // 2, rows)].reshape(rows * cols, 4 * model)
        term = dot_nn(source, weight[0])

        @pl.when(k == 0)
        def _():
            out[...] = term

        @pl.when(k != 0)
        def _():
            out[...] += term


def tail_kernel(tokens, act, w_out, cot, edge, before, after, weight):
    fine_rows, fine_cols, model = cot.shape
    width = weight.shape[1]
    count, hidden = act.shape
    block = count // 4
    whole = lambda a: pl.BlockSpec(a.shape, lambda i: (0,) * a.ndim)
    size = fine_rows * fine_cols // 4
    tokens_of = lambda w: pl.BlockSpec((block, w), lambda i: (jnp.minimum(i, 3), 0))
    return pl.pallas_call(
        tail_body,
        grid=(8,),
        in_specs=[
            tokens_of(model),
            tokens_of(hidden),
            whole(w_out),
            pl.BlockSpec(memory_space=pl.ANY),
            whole(edge),
            whole(before),
            whole(after),
            pl.BlockSpec((1, 4 * model, width), lambda i: (jnp.maximum(i - 4, 0), 0, 0)),
        ],
        out_specs=[tokens_of(model), pl.BlockSpec((size, width), lambda i: (0, 0))],
        out_shape=[
            jax.ShapeDtypeStruct((count, model), BF16),
            jax.ShapeDtypeStruct((size, width), F32),
        ],
        scratch_shapes=[
            pltpu.VMEM((fine_rows, fine_cols, model), BF16),
            pltpu.VMEM((2, fine_rows // 2 + 1, fine_cols // 2, 4 * model), BF16),
            pltpu.SemaphoreType.DMA((1,)),
        ],
        compiler_params=pltpu.CompilerParams(vmem_limit_bytes=58 << 20),
        cost_estimate=cost(7 << 30, 22 << 20),
        name="tail",
    )(tokens, act, w_out, cot, edge, before, after, weight.reshape(4, 4 * model, width))


def sum_body(parts, in_grad, out_grad):
    total = parts[0].astype(F32)
    for i in range(1, parts.shape[0]):
        total = total + parts[i].astype(F32)
    in_grad[...] = total[:64]
    packed = total[64:]
    out_grad[...] = jnp.concatenate(
        [packed, pltpu.roll(packed, 64, 1)], axis=0
    ).T[:64, :]


def sum_blocks(parts):
    return pl.pallas_call(
        sum_body,
        out_shape=[
            jax.ShapeDtypeStruct((64, 128), F32),
            jax.ShapeDtypeStruct((64, 64), F32),
        ],
        compiler_params=pltpu.CompilerParams(vmem_limit_bytes=8 << 20),
        cost_estimate=cost(1 << 20, 2 << 20),
        name="sum_blocks",
    )(parts)


def swap(last, first, axis, wrap):
    devices = lax.axis_size(axis)
    up = [(i, (i + 1) % devices) for i in range(devices if wrap else devices - 1)]
    down = [(j, i) for i, j in up]
    one = lax.ppermute(last, axis, up)
    other = lax.ppermute(first, axis, down)
    return one, other


def halos(latents, tokens, cot):
    before, after = swap(latents[-1], latents[0], "lat", False)

    def column(c):
        place = c % latents.shape[1]
        ends = [a[place : place + 1] for a in (before, after)]
        parts = [ends[0], latents[:, c], ends[1], jnp.zeros((6, latents.shape[2]), BF16)]
        for fine in (tokens, cot):
            parts.append(jnp.pad(fine[1::2, c], ((1, 7), (0, 0))))
            parts.append(jnp.pad(fine[0::2, c], ((0, 8), (0, 0))))
        return jnp.concatenate(parts, axis=0)

    left, right = swap(column(-1), column(0), "lon", True)
    return before, after, left, right


def chip_groups():
    return [
        [
            (x * 2 + y_lo) * 16 + z * 4 + y_hi * 2 + core
            for z in range(4)
            for x in range(4)
            for y_hi in range(2)
            for y_lo in range(2)
        ]
        for core in range(2)
    ]


def other_core(array):
    return lax.ppermute(array, "lon", [(i, i ^ 1) for i in range(16)])


def shards(fine_tokens, latents, upsample_weight, uniting_in, uniting_out, cotangent):
    count = fine_tokens.shape[0] * fine_tokens.shape[1]
    model = fine_tokens.shape[2]
    core = (lax.axis_index("lon") % 2).astype(jnp.int32).reshape(1)
    tokens = fine_tokens.reshape(count, model)
    cot = cotangent.reshape(count, model)

    before, after, left, right = halos(latents, fine_tokens, cotangent)
    a_own = dot_nt(cot[: count // 2], uniting_out).astype(BF16)
    act, up_cot, up_cot_edge, first_row, last_row, keep, send = main_kernel(
        core, latents, before, after, left, right, upsample_weight,
        tokens, cot, a_own, uniting_in, uniting_out,
    )
    other = other_core(send)
    above, below = swap(last_row, first_row, "lat", False)
    halves = (keep.astype(F32) + other.astype(F32)).astype(BF16).reshape(64, 96, 128)
    parts = lax.all_to_all(
        halves, BOTH, 0, 0, axis_index_groups=chip_groups(), tiled=True
    )
    united, latent_grad = tail_kernel(
        tokens, act, uniting_out, up_cot.reshape(fine_tokens.shape), up_cot_edge,
        above, below, upsample_weight,
    )
    in_grad, out_grad = sum_blocks(parts)
    return (
        united.reshape(fine_tokens.shape),
        latent_grad.reshape(latents.shape),
        in_grad,
        out_grad,
    )


def solution(mesh):
    return jax.shard_map(
        shards,
        mesh=mesh,
        in_specs=(
            P("lat", "lon", None),
            P("lat", "lon", None),
            P(),
            P(),
            P(),
            P("lat", "lon", None),
        ),
        out_specs=(P("lat", "lon", None), P("lat", "lon", None), P("lon", "lat"), P("lon", "lat")),
        check_vma=False,
    )
```
